256 devices in a mesh: ctx: 16 (over z, core), ch: 16 (over x, y).
Axes of the slice: x: 4, y: 4, z: 8, core: 2. Of those that a mesh axis runs over, the one named last changes fastest.
Arguments:
- layer_input: bfloat16 [6144, 16384], P('ctx', 'ch'), may hold values from -6 to 6
- gate_input: bfloat16 [6144, 16384], P('ctx', 'ch'), may hold values from -6 to 6
- conv_weight: float32 [4, 16384], P(None, 'ch'), may hold values from -3 to 3
- conv_bias: float32 [16384], P('ch'), may hold values from -3 to 3
- select_weight: bfloat16 [544, 16384], P(None, 'ch'), may hold values from -0.046875 to 0.046875
- step_weight: bfloat16 [512, 16384], P(None, 'ch'), may hold values from -0.25 to 0.25
- step_bias: float32 [16384], P('ch')
- decay_log: float32 [16, 16384], P(None, 'ch')
- skip_gain: float32 [16384], P('ch'), may hold values from 0.5 to 1.5
- out_weight: bfloat16 [16384, 4096], P('ch'), may hold values from -0.046875 to 0.046875
- residual: bfloat16 [6144, 4096], P('ctx', 'ch')
- norm_gain: float32 [4096], replicated, may hold values from 0.5 to 1.5
- head_weight: bfloat16 [4096, 32768], P('ctx', 'ch')
- targets: int32 [6144], P('ctx'), may hold values from 0 to 32767
Outputs:
- token_logprob: float32 [6144], P('ctx')
- mean_logprob: float32 [6144], P('ctx')
- logprob_variance: float32 [6144], P('ctx')
The draws below stay inside these ranges and needn't reach their ends.
All inputs are finite; a program needn't handle non-finite values.
Results may differ from the reference program's by a relative error of at most 0.0051.
Values may be sent and summed in bfloat16 or wider, within the bound.
A program may use at most 128 MiB of HBM per device.

```python
import math
import jax
import jax.numpy as jnp
import numpy as np
from jax import lax

D = 4096
DI = 16384
STATE = 16
RANK = 512
KCONV = 4
VOCAB = 32768
TOK_DEV = 384
TOKENS = 6144
N_CTX = 16


def channel_rates(key):
    share = 0.5
    slow_mask = jax.random.bernoulli(jax.random.fold_in(key, 41), share, (DI,))
    step_target = jnp.exp(jax.random.uniform(jax.random.fold_in(key, 42), (DI,), jnp.float32, math.log(0.02), math.log(0.2)))
    slow_rate = jnp.exp(jax.random.uniform(jax.random.fold_in(key, 43), (DI,), jnp.float32, math.log(0.1), math.log(0.5))) / TOKENS
    fast_rate = jnp.exp(jax.random.uniform(jax.random.fold_in(key, 44), (DI,), jnp.float32, math.log(1.0 / 50.0), math.log(1.0 / 30.0)))
    rate_target = jnp.where(slow_mask, slow_rate, fast_rate)
    return (step_target, rate_target)


def draw_step_bias(key, part):
    step_target, rate_target = channel_rates(key)
    return jnp.log(jnp.expm1(step_target))


def draw_decay_log(key, part):
    step_target, rate_target = channel_rates(key)
    jitter = jax.random.uniform(jax.random.fold_in(key, 45), (STATE, DI), jnp.float32, -0.7, 0.7)
    return jnp.log(rate_target[None, :] / step_target[None, :]) + jitter


def draw_residual(key, part):
    ramp = 1.0 + 2.0 * jnp.arange(D, dtype=jnp.float32) / (D - 1)
    base = jax.random.normal(jax.random.fold_in(key, 52), (TOKENS, D), jnp.float32)
    return (base * ramp[None, :]).astype(jnp.bfloat16)


def draw_head_weight(key, part):
    scale = 3.0 / math.sqrt(D)
    weights = jnp.clip(jax.random.normal(jax.random.fold_in(key, 61), (D, VOCAB), jnp.float32), -4.0, 4.0) * scale
    return weights.astype(jnp.bfloat16)


def plant(entries, rng, least, top_value):
    index_at = [jax.random.randint(jax.random.fold_in(rng, axis), (), 0, length) for axis, length in enumerate(entries.shape)]
    longest = entries.shape.index(max(entries.shape))
    neighbour = index_at[:longest] + [(index_at[longest] + 1) % entries.shape[longest]] + index_at[longest + 1:]
    return entries.at[tuple(index_at)].set(least).at[tuple(neighbour)].set(top_value)


def block_scale(rng, dims, shards, smallest, top_value):
    level = 1.0
    for position, parts in shards:
        steps = jax.random.uniform(jax.random.fold_in(jax.random.fold_in(rng, 6), position), (parts,), jnp.float32, smallest / len(shards), top_value / len(shards))
        level = level * jnp.repeat(jnp.exp(steps), dims[position] // parts).reshape((-1,) + (1,) * (len(dims) - 1 - position))
    return level


def cumulative_ranks(amount, skew):
    portions = [(1 << 20) // math.isqrt(standing ** skew) + 1 for standing in range(1, amount + 1)]
    scale = 1 + sum(portions) // (1 << 30)
    return np.cumsum(np.array([max(1, weight // scale) for weight in portions]))


def ranked(stream_key, dims, count, slope):
    listing = cumulative_ranks(count, slope)
    lot = jax.random.randint(jax.random.fold_in(stream_key, 1), dims, 0, int(listing[count - 1]))
    standing = jnp.searchsorted(jnp.asarray(listing, jnp.int32), lot, side="right")
    return jax.random.permutation(jax.random.fold_in(stream_key, 2), count)[standing].astype(jnp.int32)


def bell_draw(rng, extent, scale, most, cuts=(), kind=jnp.bfloat16):
    values = jax.random.normal(rng, extent, jnp.float32) * scale
    if len(cuts) > 0:
        values = block_scale(rng, extent, cuts, -0.22, 0.18) * values
    return jnp.clip(values, min=-most, max=most).astype(kind)


def setup_inputs(seed: int = 0) -> dict:
    seeds = jax.random.split(jax.random.key(seed), 15)
    layer_input = bell_draw(seeds[0], (TOKENS, DI), 1.0, 6.0, ((0, 16), (1, 16)))
    gate_input = bell_draw(seeds[1], (TOKENS, DI), 1.0, 6.0, ((0, 16), (1, 16)))
    conv_weight = bell_draw(seeds[2], (KCONV, DI), KCONV ** -0.5, 3.0, ((1, 16),), jnp.float32)
    conv_bias = bell_draw(seeds[3], (DI,), 0.5, 3.0, ((0, 16),), jnp.float32)
    select_weight = bell_draw(seeds[4], (RANK + 2 * STATE, DI), DI ** -0.5, 0.046875, ((1, 16),))
    step_weight = bell_draw(seeds[5], (RANK, DI), RANK ** -0.5, 0.25, ((1, 16),))
    step_bias = draw_step_bias(jax.random.fold_in(seeds[14], 71), 0)
    decay_log = draw_decay_log(jax.random.fold_in(seeds[14], 71), 0)
    skip_gain = jnp.clip(0.5 + 1.0 * jax.random.uniform(seeds[8], (DI,), jnp.float32) ** block_scale(seeds[8], (DI,), ((0, 16),), -0.2, 0.2), 0.5, 1.5)
    out_weight = bell_draw(seeds[9], (DI, D), DI ** -0.5, 0.046875, ((0, 16),))
    residual = draw_residual(jax.random.fold_in(seeds[14], 71), 0)
    norm_gain = jnp.clip(1.0 + 0.1 * jax.random.normal(seeds[11], (D,), jnp.float32), 0.5, 1.5)
    head_weight = draw_head_weight(jax.random.fold_in(seeds[14], 71), 0)
    targets = plant(ranked(seeds[13], (TOKENS,), VOCAB, 2), jax.random.fold_in(seeds[13], 3), 0, VOCAB - 1).astype(jnp.int32)
    return {"layer_input": layer_input, "gate_input": gate_input, "conv_weight": conv_weight, "conv_bias": conv_bias, "select_weight": select_weight, "step_weight": step_weight, "step_bias": step_bias, "decay_log": decay_log, "skip_gain": skip_gain, "out_weight": out_weight, "residual": residual, "norm_gain": norm_gain, "head_weight": head_weight, "targets": targets}


def sigmoid_linear(operand):
    return operand / (1.0 + jnp.exp(-operand))

def smooth_relu(operand):
    return jnp.logaddexp(operand, 0.0)

def reference(layer_input, gate_input, conv_weight, conv_bias, select_weight, step_weight, step_bias, decay_log, skip_gain, out_weight, residual, norm_gain, head_weight, targets):
    widened = layer_input.astype(jnp.float32)
    padded = jnp.concatenate([jnp.zeros((KCONV - 1, DI), jnp.float32), widened], axis=0)
    convolved = jnp.zeros((TOKENS, DI), jnp.float32) + conv_bias[None, :]
    for offset in range(KCONV):
        convolved = convolved + conv_weight[offset][None, :] * padded[offset:offset + TOKENS]
    smoothed = sigmoid_linear(convolved).astype(jnp.bfloat16)
    projected = lax.dot_general(select_weight, smoothed, (((1,), (1,)), ((), ())), preferred_element_type=jnp.float32)
    step_low = projected[:RANK].astype(jnp.bfloat16)
    state_entry = projected[RANK:RANK + STATE]
    state_readout = projected[RANK + STATE:]
    step_raw = lax.dot_general(step_low, step_weight, (((0,), (0,)), ((), ())), preferred_element_type=jnp.float32)
    step_size = smooth_relu(step_raw + step_bias[None, :])
    decay_rate = -jnp.exp(decay_log)
    smoothed_wide = smoothed.astype(jnp.float32)

    def advance(state_now, inputs):
        size_now, value_now, entry_now, readout_now = inputs
        state_now = jnp.exp(size_now[None, :] * decay_rate) * state_now + (size_now * value_now)[None, :] * entry_now[:, None]
        return (state_now, lax.optimization_barrier(jnp.sum(readout_now[:, None] * state_now, axis=0)))
    final_state, scanned = lax.scan(advance, jnp.zeros((STATE, DI), jnp.float32), (step_size, smoothed_wide, state_entry.T, state_readout.T))
    mixer_input = ((scanned + skip_gain[None, :] * smoothed_wide) * sigmoid_linear(gate_input.astype(jnp.float32))).astype(jnp.bfloat16)
    mixer_out = jnp.dot(mixer_input, out_weight, preferred_element_type=jnp.float32)
    hidden = residual.astype(jnp.float32) + mixer_out
    mean_square = lax.optimization_barrier(lax.optimization_barrier(jnp.mean(hidden * hidden, axis=1, keepdims=True)))
    normed = (hidden * lax.rsqrt(mean_square + 1e-06) * norm_gain[None, :]).astype(jnp.bfloat16)

    def score_block(block):
        row_block, wanted = block
        logits = jnp.dot(row_block, head_weight, preferred_element_type=jnp.float32)
        row_peak = lax.optimization_barrier(jnp.max(logits, axis=1))
        shifted = logits - row_peak[:, None]
        weights = jnp.exp(shifted)
        row_total = lax.optimization_barrier(jnp.sum(weights, axis=1))
        row_first = lax.optimization_barrier(jnp.sum(weights * shifted, axis=1))
        row_second = lax.optimization_barrier(jnp.sum(weights * shifted * shifted, axis=1))
        column = lax.broadcasted_iota(jnp.int32, logits.shape, 1)
        picked = lax.optimization_barrier(jnp.sum(jnp.where(column == wanted[:, None], logits, 0.0), axis=1))
        log_total = jnp.log(row_total)
        mean_ratio = row_first / row_total
        return (picked - row_peak - log_total, mean_ratio - log_total, row_second / row_total - mean_ratio * mean_ratio)
    blocks = (normed.reshape(N_CTX, TOK_DEV, D), targets.reshape(N_CTX, TOK_DEV))
    logprob, mean_part, variance = lax.map(score_block, blocks)
    return (logprob.reshape(TOKENS), mean_part.reshape(TOKENS), variance.reshape(TOKENS))
```

```python
import functools

import jax
import jax.numpy as jnp
from jax import lax
from jax.experimental import pallas as pl
from jax.experimental.pallas import tpu as pltpu
from jax.sharding import PartitionSpec as P

STATE = 16
RANK = 512
KCONV = 4
TOK = 384
CH = 1024
D = 4096
VOC = 2048
NCH = 16
NZ = 8
LOG2E = 1.4426950408889634
MESH = pl.DeviceIdType.MESH
F32 = jnp.float32
BF16 = jnp.bfloat16
VM = pl.BlockSpec(memory_space=pltpu.VMEM)
SM = pl.BlockSpec(memory_space=pltpu.SMEM)
HBM = pl.BlockSpec(memory_space=pl.ANY)


def params(**kw):
    return pltpu.CompilerParams(vmem_limit_bytes=60 * 1024 * 1024, **kw)


def greet(peers):
    barrier = pltpu.get_barrier_semaphore()
    for peer in peers:
        pl.semaphore_signal(barrier, inc=1, device_id=peer, device_id_type=MESH)
    pl.semaphore_wait(barrier, len(peers))


def remote(src, dst, send_sem, recv_sem, peer):
    return pltpu.make_async_remote_copy(
        src_ref=src, dst_ref=dst, send_sem=send_sem, recv_sem=recv_sem, device_id=peer, device_id_type=MESH
    )


def sigmoid_linear(operand):
    return operand / (1.0 + jnp.exp(-operand))


ROWS = RANK // NCH


def sum_projected_kernel(part, bcpart, out, bc, recv, mine, recvx, minex, s1, r1, s2, r2, sx, rx, sy, ry):
    me = lax.axis_index("ch")
    others = [lax.rem(me + off, NCH) for off in range(1, NCH)]
    greet([{"ch": p} for p in others])
    first = []
    for k, p in enumerate(others):
        rows = pl.ds(pl.multiple_of(p * ROWS, ROWS), ROWS)
        c = remote(part.at[rows], recv.at[k], s1.at[k], r1.at[k], {"ch": p})
        c.start()
        first.append(c)

    def tile(k):
        slot = lax.rem(me - 5 * k + 2 * NCH, NCH) - 1
        return remote(bcpart.at[pl.ds(8 * k, 8)], recvx.at[slot], sx.at[k], rx.at[slot], {"ch": 5 * k})

    for k in range(4):
        @pl.when(me != 5 * k)
        def _():
            tile(k).start()

    myrows = pl.ds(pl.multiple_of(me * ROWS, ROWS), ROWS)
    for c in first:
        c.wait_recv()
    total = part[myrows].astype(F32)
    for k in range(NCH - 1):
        total = total + recv[k].astype(F32)
    mine[...] = total.astype(BF16)
    second = []
    for k, p in enumerate(others):
        c = remote(mine, out.at[myrows], s2.at[k], r2.at[k], {"ch": p})
        c.start()
        second.append(c)
    out[myrows] = mine[...]
    for k in range(4):
        def spread(j):
            return remote(minex, bc.at[pl.ds(8 * k, 8)], sy.at[j], ry.at[k], {"ch": lax.rem(me + j + 1, NCH)})

        @pl.when(me == 5 * k)
        def _():
            sumx = bcpart[8 * k : 8 * k + 8]
            for j in range(NCH - 1):
                remote(minex, recvx.at[j], sx.at[0], rx.at[j], {"ch": others[0]}).wait_recv()
                sumx = sumx + recvx[j]
            minex[...] = sumx
            for j in range(NCH - 1):
                spread(j).start()
            bc[8 * k : 8 * k + 8] = minex[...]

    for k in range(4):
        @pl.when(me != 5 * k)
        def _():
            tile(k).wait_send()
            remote(minex, bc.at[pl.ds(8 * k, 8)], sy.at[0], ry.at[k], {"ch": 5 * k}).wait_recv()

        @pl.when(me == 5 * k)
        def _():
            for j in range(NCH - 1):
                remote(minex, bc.at[pl.ds(8 * k, 8)], sy.at[j], ry.at[k], {"ch": others[j]}).wait_send()

    for c in second:
        c.wait_recv()
    for c in first:
        c.wait_send()
    for c in second:
        c.wait_send()


def sum_projected(part, bcpart):
    n = NCH - 1
    dma = pltpu.SemaphoreType.DMA
    return pl.pallas_call(
        sum_projected_kernel,
        out_shape=(jax.ShapeDtypeStruct(part.shape, BF16), jax.ShapeDtypeStruct(bcpart.shape, F32)),
        in_specs=[VM, VM],
        out_specs=(VM, VM),
        scratch_shapes=[
            pltpu.VMEM((n, ROWS, TOK), BF16),
            pltpu.VMEM((ROWS, TOK), BF16),
            pltpu.VMEM((n, 8, TOK), F32),
            pltpu.VMEM((8, TOK), F32),
            dma((n,)), dma((n,)), dma((n,)), dma((n,)), dma((4,)), dma((n,)), dma((n,)), dma((4,)),
        ],
        compiler_params=params(collective_id=0, has_side_effects=True),
        name="sum_projected",
    )(part, bcpart)


NTB = TOK // 8
FLAT = NTB * 64


def to_flat(ref, value, tok0):
    rows = value.shape[0]
    for b in range(rows // 8):
        for lt in range(8):
            start = (tok0 // 8 + b) * 64 + lt * 8
            ref[start : start + 8, :] = value[8 * b : 8 * b + 8, 128 * lt : 128 * lt + 128]


def scan_kernel(proj, step_w, bias, decay, smoothed, bc, y_out, e_out, state_out, total_out, dtf, uf):
    for k in range(TOK // 128):
        tok0 = 128 * k
        low = proj[:, tok0 : tok0 + 128]
        raw = lax.dot_general(low, step_w[...], (((0,), (0,)), ((), ())), preferred_element_type=F32)
        v = raw + bias[...]
        dt = jnp.maximum(v, 0.0) + jnp.log1p(jnp.exp(-jnp.abs(v)))
        to_flat(dtf, dt, tok0)
        to_flat(uf, dt * smoothed[tok0 : tok0 + 128, :].astype(F32), tok0)
    rates = [-jnp.exp(decay[8 * n : 8 * n + 8, :]) * LOG2E for n in range(STATE)]

    def block(tb, carry):
        state, elapsed = list(carry[:STATE]), carry[STATE]
        for r in range(8):
            rows = pl.ds(tb * 64 + r, 8, stride=8)
            dt = dtf[rows, :]
            u = uf[rows, :]
            t = tb * 8 + r
            y = None
            for n in range(STATE):
                state[n] = jnp.exp2(dt * rates[n]) * state[n] + u * bc[n, t]
                term = state[n] * bc[STATE + n, t]
                y = term if y is None else y + term
            elapsed = elapsed + dt
            y_out[rows, :] = y
            e_out[rows, :] = elapsed
        return (*state, elapsed)

    zero = jnp.zeros((8, 128), F32)
    last = lax.fori_loop(0, NTB, block, (zero,) * (STATE + 1))
    for n in range(STATE):
        state_out[8 * n : 8 * n + 8, :] = last[n]
    total_out[...] = last[STATE]


def local_scan(proj, step_w, bias, decay, smoothed, bc):
    shape = jax.ShapeDtypeStruct
    return pl.pallas_call(
        scan_kernel,
        out_shape=(shape((FLAT, 128), F32), shape((FLAT, 128), F32), shape((STATE * 8, 128), F32), shape((8, 128), F32)),
        in_specs=[VM, VM, VM, VM, VM, SM],
        out_specs=(VM, VM, VM, VM),
        scratch_shapes=[pltpu.VMEM((FLAT, 128), F32), pltpu.VMEM((FLAT, 128), F32)],
        compiler_params=params(),
        name="local_scan",
    )(proj, step_w, bias, decay, smoothed, bc)


HALF = STATE * 4


def carry_kernel(state, total, decay, out, swap_s, swap_e, got_s, got_e, send_s, send_e, zs, ze, hold, fin, ss, rs, sz, rz, sf, rf):
    me = lax.axis_index("ctx")
    z = me // 2
    c = lax.rem(me, 2)
    partner = {"ctx": z * 2 + 1 - c}
    greet([partner] + [{"ctx": lax.rem(z + d, NZ) * 2 + c} for d in range(1, NZ)])
    mine = pl.ds(pl.multiple_of(c * HALF, HALF), HALF)
    other = pl.ds(pl.multiple_of((1 - c) * HALF, HALF), HALF)
    swap_s[...] = state[other, :]
    swap_e[...] = total[...]
    a = remote(swap_s, got_s, ss.at[0], rs.at[0], partner)
    b = remote(swap_e, got_e, ss.at[1], rs.at[1], partner)
    a.start()
    b.start()
    rate = -jnp.exp(decay[mine, :]) * LOG2E

    def through(elapsed):
        return jnp.exp2(rate * jnp.tile(elapsed, (HALF // 8, 1)))

    a.wait_recv()
    b.wait_recv()
    own_s, own_e, oth_s, oth_e = state[mine, :], total[...], got_s[...], got_e[...]
    low = c == 0
    s0, s1 = jnp.where(low, own_s, oth_s), jnp.where(low, oth_s, own_s)
    e0, e1 = jnp.where(low, own_e, oth_e), jnp.where(low, oth_e, own_e)
    send_s[...] = (through(e1) * s0 + s1).astype(BF16)
    send_e[...] = e0 + e1

    def pair(d):
        peer = {"ctx": (z + d) * 2 + c}
        return (
            remote(send_s, zs.at[d - 1], sz.at[0, d - 1], rz.at[0, d - 1], peer),
            remote(send_e, ze.at[d - 1], sz.at[1, d - 1], rz.at[1, d - 1], peer),
        )

    def incoming(d):
        peer = {"ctx": (z - d) * 2 + c}
        return (
            remote(send_s, zs.at[d - 1], sz.at[0, d - 1], rz.at[0, d - 1], peer),
            remote(send_e, ze.at[d - 1], sz.at[1, d - 1], rz.at[1, d - 1], peer),
        )

    for d in range(1, NZ):
        @pl.when(z + d < NZ)
        def _():
            for copy in pair(d):
                copy.start()

    hold[...] = jnp.zeros_like(hold)
    for d in range(NZ - 1, 0, -1):
        @pl.when(z >= d)
        def _():
            for copy in incoming(d):
                copy.wait_recv()
            hold[...] = through(ze[d - 1]) * hold[...] + zs[d - 1].astype(F32)

    into0 = hold[...]
    into1 = through(e0) * into0 + s0
    fin[...] = jnp.where(low, into1, into0)
    out[mine, :] = jnp.where(low, into0, into1)
    f = remote(fin, out.at[mine], sf.at[0], rf.at[0], partner)
    f.start()
    f.wait_recv()
    f.wait_send()
    a.wait_send()
    b.wait_send()
    for d in range(1, NZ):
        @pl.when(z + d < NZ)
        def _():
            for copy in pair(d):
                copy.wait_send()


def carry_in(state, total, decay):
    dma = pltpu.SemaphoreType.DMA
    return pl.pallas_call(
        carry_kernel,
        out_shape=jax.ShapeDtypeStruct((STATE * 8, 128), F32),
        in_specs=[VM, VM, VM],
        out_specs=VM,
        scratch_shapes=[
            pltpu.VMEM((HALF, 128), F32),
            pltpu.VMEM((8, 128), F32),
            pltpu.VMEM((HALF, 128), F32),
            pltpu.VMEM((8, 128), F32),
            pltpu.VMEM((HALF, 128), BF16),
            pltpu.VMEM((8, 128), F32),
            pltpu.VMEM((NZ - 1, HALF, 128), BF16),
            pltpu.VMEM((NZ - 1, 8, 128), F32),
            pltpu.VMEM((HALF, 128), F32),
            pltpu.VMEM((HALF, 128), F32),
            dma((2,)), dma((2,)), dma((2, NZ - 1)), dma((2, NZ - 1)), dma((1,)), dma((1,)),
        ],
        compiler_params=params(collective_id=1, has_side_effects=True),
        name="carry_in",
    )(state, total, decay)


def gate_kernel(y, e, incoming, decay, bc, smoothed, gate, skip, out, zf):
    rates = [-jnp.exp(decay[8 * n : 8 * n + 8, :]) * LOG2E for n in range(STATE)]
    into = [incoming[8 * n : 8 * n + 8, :] for n in range(STATE)]

    def block(tb, _):
        for r in range(8):
            rows = pl.ds(tb * 64 + r, 8, stride=8)
            elapsed = e[rows, :]
            total = y[rows, :]
            t = tb * 8 + r
            for n in range(STATE):
                total = total + jnp.exp2(elapsed * rates[n]) * into[n] * bc[STATE + n, t]
            zf[rows, :] = total
        return 0

    lax.fori_loop(0, NTB, block, 0)
    for k in range(TOK // 16):
        rows = slice(16 * k, 16 * k + 16)
        for lt in range(8):
            lanes = slice(128 * lt, 128 * lt + 128)
            start = (2 * k) * 64 + lt * 8
            scanned = jnp.concatenate([zf[start : start + 8, :], zf[start + 64 : start + 72, :]], axis=0)
            value = scanned + skip[:, lanes] * smoothed[rows, lanes].astype(F32)
            out[rows, lanes] = (value * sigmoid_linear(gate[rows, lanes].astype(F32))).astype(BF16)


def gated(y, e, incoming, decay, bc, smoothed, gate, skip):
    return pl.pallas_call(
        gate_kernel,
        out_shape=jax.ShapeDtypeStruct((TOK, CH), BF16),
        in_specs=[VM, VM, VM, VM, SM, VM, VM, VM],
        out_specs=VM,
        scratch_shapes=[pltpu.VMEM((FLAT, 128), F32)],
        compiler_params=params(),
        name="gated",
    )(y, e, incoming, decay, bc, smoothed, gate, skip)


NQ = 4
QR = TOK // NQ
BLK = D // NCH


def cube_of(index):
    x, y = index // 4, lax.rem(index, 4)
    return [lax.rem(x + x // 2, 2), x // 2, lax.rem(y + y // 2, 2), y // 2]


def index_of(bits):
    def line(low, high):
        return high * 2 + lax.rem(high + low, 2)

    return line(bits[0], bits[1]) * 4 + line(bits[2], bits[3])


def mix_kernel(mixer, weight, residual, gain, out, wv, acc, part, got, ws, s1, r1, s2, r2):
    me = lax.axis_index("ch")
    bits = cube_of(me)

    def block(r):
        return index_of([lax.rem(bits[d] + ((r >> d) & 1), 2) for d in range(4)])

    def lanes(r):
        return pl.ds(pl.multiple_of(block(r) * BLK, BLK), BLK)

    order = [15, 14, 13, 11, 7, 12, 10, 9, 6, 5, 3, 8, 4, 2, 1, 0]
    loads = []
    for k in range(8):
        piece = pl.ds(CH // 8 * k, CH // 8)
        loads.append(pltpu.make_async_copy(weight.at[piece], wv.at[piece], ws.at[k]))
        loads[k].start()
    peers = [{"ch": block(1 << d)} for d in range(4)]
    greet(peers)

    def rows(q):
        return pl.ds(QR * q, QR)

    def dim(q, s):
        return (q + s) % 4

    def kept(q, s):
        return [r for r in range(16) if all(not (r >> dim(q, i)) & 1 for i in range(s))]

    sent = []

    def send(q, s, r):
        d = dim(q, s)
        c = remote(
            part.at[r, rows(q)], got.at[s, r ^ (1 << d), rows(q)], s1.at[r, q], r1.at[q, r ^ (1 << d), s], peers[d]
        )
        c.start()
        sent.append(c)

    def take(q, s, r):
        d = dim(q, s)
        remote(part.at[r, rows(q)], got.at[s, r, rows(q)], s1.at[r, q], r1.at[q, r, s], peers[d]).wait_recv()

    for load in loads:
        load.wait()
    for r in order:
        product = jnp.dot(mixer[...], wv[:, lanes(r)], preferred_element_type=F32)
        acc[r] = product
        part[r] = product.astype(BF16)
        for q in range(NQ):
            if (r >> dim(q, 0)) & 1:
                send(q, 0, r)
    for s in range(3):
        for q in range(NQ):
            left = kept(q, s + 1)
            d = dim(q, s + 1)
            for r in [r for r in left if (r >> d) & 1] + [r for r in left if not (r >> d) & 1]:
                take(q, s, r)
                total = acc[r, rows(q)] + got[s, r, rows(q)].astype(F32)
                if not (r >> d) & 1:
                    acc[r, rows(q)] = total
                else:
                    part[r, rows(q)] = total.astype(BF16)
                    send(q, s + 1, r)

    def give(q, s, r):
        d = dim(q, s)
        where = out.at[rows(q), lanes(r)]
        return remote(where, where, s2.at[q, s, r], r2.at[q, s, r ^ (1 << d)], peers[d])

    def spread(q, s):
        held = [0]
        for i in range(s):
            held = held + [r ^ (1 << dim(q, i)) for r in held]
        return held

    for q in range(NQ):
        take(q, 3, 0)
        total = acc[0, rows(q)] + got[3, 0, rows(q)].astype(F32)
        hidden = residual[rows(q), :].astype(F32) + total
        out[rows(q), lanes(0)] = (hidden * gain[:, lanes(0)]).astype(BF16)
        c = give(q, 0, 0)
        c.start()
        sent.append(c)

    def arrived(q, s, r):
        where = out.at[rows(q), lanes(r)]
        remote(where, where, s2.at[q, s, r], r2.at[q, s, r], peers[dim(q, s)]).wait_recv()

    for s in range(4):
        for q in range(NQ):
            for r in spread(q, s):
                arrived(q, s, r ^ (1 << dim(q, s)))
            if s < 3:
                for r in spread(q, s + 1):
                    c = give(q, s + 1, r)
                    c.start()
                    sent.append(c)
    for c in sent:
        c.wait_send()


def mix(mixer, weight, residual, gain):
    dma = pltpu.SemaphoreType.DMA
    return pl.pallas_call(
        mix_kernel,
        out_shape=jax.ShapeDtypeStruct((TOK, D), BF16),
        in_specs=[VM, HBM, VM, VM],
        out_specs=VM,
        scratch_shapes=[
            pltpu.VMEM((CH, D), BF16),
            pltpu.VMEM((NCH, TOK, BLK), F32),
            pltpu.VMEM((NCH, TOK, BLK), BF16),
            pltpu.VMEM((4, NCH, TOK, BLK), BF16),
            dma((8,)),
            dma((NCH, NQ)),
            dma((NQ, NCH, 4)),
            dma((NQ, 4, NCH)),
            dma((NQ, 4, NCH)),
        ],
        compiler_params=params(collective_id=2, has_side_effects=True),
        name="mix",
    )(mixer, weight, residual, gain)


VT = 256
NVT = VOC // VT


def score_kernel(scaled, head, gain, targets, out, logits, rms):
    step = pl.program_id(0)

    @pl.when(step == 0)
    def _():
        acc = jnp.zeros((TOK, BLK), F32)
        for k in range(D // BLK):
            lanes = slice(BLK * k, BLK * k + BLK)
            h = scaled[:, lanes].astype(F32) / gain[:, lanes]
            acc = acc + h * h
        mean = jnp.sum(acc, axis=1, keepdims=True) * (1.0 / D)
        rms[...] = lax.rsqrt(mean + 1e-06)

    logits[step] = jnp.dot(scaled[...], head[...], preferred_element_type=F32) * rms[...]

    @pl.when(step == NVT - 1)
    def _():
        first = lax.axis_index("ch") * VOC
        lane = lax.broadcasted_iota(jnp.int32, (32, VT), 1)
        place = lax.broadcasted_iota(jnp.int32, (32, 128), 1)
        for k in range(TOK // 32):
            rows = slice(32 * k, 32 * k + 32)
            values = [logits[j, rows] for j in range(NVT)]
            peak = values[0]
            for v in values[1:]:
                peak = jnp.maximum(peak, v)
            peak = jnp.max(peak, axis=1, keepdims=True)
            want = targets[rows, :] - first
            sums = [jnp.zeros((32, VT), F32) for _ in range(4)]
            for j, v in enumerate(values):
                shifted = v - peak
                w = jnp.exp(shifted)
                ws = w * shifted
                sums[0] = sums[0] + w
                sums[1] = sums[1] + ws
                sums[2] = sums[2] + ws * shifted
                sums[3] = sums[3] + jnp.where(lane + j * VT == want, v, 0.0)
            cols = [peak] + [jnp.sum(v, axis=1, keepdims=True) for v in sums]
            packed = jnp.zeros((32, 128), F32)
            for i, v in enumerate(cols):
                packed = jnp.where(place == i, v, packed)
            out[rows, :] = packed


def score(scaled, head, gain, targets):
    return pl.pallas_call(
        score_kernel,
        out_shape=jax.ShapeDtypeStruct((TOK, 128), F32),
        grid=(NVT,),
        in_specs=[
            pl.BlockSpec((TOK, D), lambda i: (0, 0)),
            pl.BlockSpec((D, VT), lambda i: (0, i)),
            pl.BlockSpec((1, D), lambda i: (0, 0)),
            pl.BlockSpec((TOK, 1), lambda i: (0, 0)),
        ],
        out_specs=pl.BlockSpec((TOK, 128), lambda i: (0, 0)),
        scratch_shapes=[pltpu.VMEM((NVT, TOK, VT), F32), pltpu.VMEM((TOK, 1), F32)],
        compiler_params=params(),
        name="score",
    )(scaled, head, gain, targets)


def combine_kernel(packed, out, mine, got, ss, rs):
    me = lax.axis_index("ch")
    others = [lax.rem(me + off, NCH) for off in range(1, NCH)]
    mine[...] = jnp.transpose(packed[...])[:8, :]
    greet([{"ch": p} for p in others])
    copies = []
    for k, p in enumerate(others):
        c = remote(mine, got.at[k], ss.at[k], rs.at[k], {"ch": p})
        c.start()
        copies.append(c)
    for c in copies:
        c.wait_recv()
    parts = [mine[...]] + [got[k] for k in range(NCH - 1)]
    peak = parts[0][0:1, :]
    for v in parts[1:]:
        peak = jnp.maximum(peak, v[0:1, :])
    total = first = second = picked = jnp.zeros((1, TOK), F32)
    for v in parts:
        d = v[0:1, :] - peak
        w = jnp.exp(d)
        wd = w * d
        total = total + w * v[1:2, :]
        first = first + (w * v[2:3, :] + wd * v[1:2, :])
        second = second + (w * v[3:4, :] + 2.0 * wd * v[2:3, :] + wd * d * v[1:2, :])
        picked = picked + v[4:5, :]
    log_total = jnp.log(total)
    ratio = first / total
    out[0:1, :] = picked - peak - log_total
    out[1:2, :] = ratio - log_total
    out[2:3, :] = second / total - ratio * ratio
    for c in copies:
        c.wait_send()


def combine(packed):
    dma = pltpu.SemaphoreType.DMA
    return pl.pallas_call(
        combine_kernel,
        out_shape=jax.ShapeDtypeStruct((8, TOK), F32),
        in_specs=[VM],
        out_specs=VM,
        scratch_shapes=[
            pltpu.VMEM((8, TOK), F32),
            pltpu.VMEM((NCH - 1, 8, TOK), F32),
            dma((NCH - 1,)),
            dma((NCH - 1,)),
        ],
        compiler_params=params(collective_id=3, has_side_effects=True),
        name="combine",
    )(packed)


def per_device(
    layer_input, gate_input, conv_weight, conv_bias, select_weight, step_weight, step_bias, decay_log,
    skip_gain, out_weight, residual, norm_gain, head_weight, targets,
):
    head = lax.all_gather(head_weight, "ctx", axis=0, tiled=True)
    size = lax.axis_size("ctx")
    edge = lax.ppermute(layer_input[TOK - (KCONV - 1) :], "ctx", [(i, i + 1) for i in range(size - 1)])
    padded = jnp.concatenate([edge, layer_input], axis=0).astype(F32)
    convolved = jnp.zeros((TOK, CH), F32) + conv_bias[None, :]
    for offset in range(KCONV):
        convolved = convolved + conv_weight[offset][None, :] * padded[offset : offset + TOK]
    smoothed = sigmoid_linear(convolved).astype(BF16)
    part = lax.dot_general(select_weight, smoothed, (((1,), (1,)), ((), ())), preferred_element_type=F32)
    proj, bc = sum_projected(part[:RANK].astype(BF16), part[RANK:])
    decay = decay_log.reshape(STATE * 8, 128)
    y, e, state, total = local_scan(proj, step_weight, step_bias[None, :], decay, smoothed, bc)
    incoming = carry_in(state, total, decay)
    mixer = gated(y, e, incoming, decay, bc, smoothed, gate_input, skip_gain[None, :])
    scaled = mix(mixer, out_weight, residual, norm_gain[None, :])
    packed = score(scaled, head, norm_gain[None, :], targets[:, None])
    result = combine(packed)
    return result[0], result[1], result[2]


def solution(mesh):
    in_specs = (
        P("ctx", "ch"), P("ctx", "ch"), P(None, "ch"), P("ch"), P(None, "ch"), P(None, "ch"), P("ch"),
        P(None, "ch"), P("ch"), P("ch", None), P("ctx", "ch"), P(), P("ctx", "ch"), P("ctx"),
    )
    return jax.shard_map(
        per_device, mesh=mesh, in_specs=in_specs, out_specs=(P("ctx"), P("ctx"), P("ctx")), check_vma=False
    )
```

```python
import jax
import jax.numpy as jnp
from jax import lax
from jax.experimental import pallas as pl
from jax.experimental.pallas import tpu as pltpu
from jax.sharding import PartitionSpec as P

STATE = 16
RANK = 512
KCONV = 4
TOK = 384
CH = 1024
D = 4096
VOC = 2048
NCH = 16
NCTX = 16
NZ = 8
NT = 3
TC = TOK // NT
ROWS = RANK // NCH
NTB = TOK // 8
FLAT = NTB * 64
HALF = STATE * 4
NQ = 4
QR = TOK // NQ
BLK = D // NCH
HB = D // NCTX
HP = HB // 2
VT = 256
NVT = VOC // VT
MESH = pl.DeviceIdType.MESH
F32 = jnp.float32
BF16 = jnp.bfloat16
VM = pl.BlockSpec(memory_space=pltpu.VMEM)
HBM = pl.BlockSpec(memory_space=pl.ANY)
SLOT = (0, 8, 12, 14)


def remote(src, dst, send_sem, recv_sem, peer):
    return pltpu.make_async_remote_copy(
        src_ref=src, dst_ref=dst, send_sem=send_sem, recv_sem=recv_sem, device_id=peer, device_id_type=MESH
    )


def sigmoid_linear(operand):
    return operand / (1.0 + jnp.exp(-operand))


def cube_of(index):
    x, y = index // 4, lax.rem(index, 4)
    return [lax.rem(x + x // 2, 2), x // 2, lax.rem(y + y // 2, 2), y // 2]


def index_of(bits):
    def line(low, high):
        return high * 2 + lax.rem(high + low, 2)

    return line(bits[0], bits[1]) * 4 + line(bits[2], bits[3])


def kernel(
    xin, gate_in, select_in, stepw_in, outw_in, head_in, residual, conv_w, conv_b, step_b, decay_in, skip, gain, targets,
    out,
    xs, gs, sel, stepw, wv, head, halo, xpad, sm, sg, dflat, pb, bcp, recv, mine, proj, recvx, minex, bc, bb,
    dtf, uf, state, total, swap_s, got_s, got_e, send_s, send_e, zs, ze, hold, fin, into,
    mixer, acc, part, got, scaled, rms, tcol, stat, gstat,
    ld, hs, hr, hps, hpr, halos, halor, s1, r1, s2, r2, sx, rx, sy, ry, cs, cr, csz, crz, csf, crf, ms, mr, gsn, grv, es, er,
):
    ch = lax.axis_index("ch")
    ctx = lax.axis_index("ctx")
    z, c = ctx // 2, lax.rem(ctx, 2)
    pending = []

    def begin(copy):
        copy.start()
        pending.append(copy)
        return copy

    others = [lax.rem(ch + off, NCH) for off in range(1, NCH)]
    partner = {"ctx": z * 2 + 1 - c}
    after, before = lax.rem(ctx + 1, NCTX), lax.rem(ctx + NCTX - 1, NCTX)
    cross = jnp.where(c == 0, before, after)
    greeted = [{"ch": p} for p in others] + [partner, {"ctx": cross}]
    greeted += [{"ctx": lax.rem(z + d, NZ) * 2 + c} for d in range(1, NZ)]
    barrier = pltpu.get_barrier_semaphore()
    for peer in greeted:
        pl.semaphore_signal(barrier, inc=1, device_id=peer, device_id_type=MESH)

    own = pl.ds(pl.multiple_of(ctx * HB, HB), HB)
    local = [
        pltpu.make_async_copy(xin, xs, ld.at[0]),
        pltpu.make_async_copy(select_in, sel, ld.at[1]),
        pltpu.make_async_copy(stepw_in, stepw, ld.at[2]),
        pltpu.make_async_copy(gate_in, gs, ld.at[3]),
        pltpu.make_async_copy(head_in, head.at[own], ld.at[4]),
        pltpu.make_async_copy(outw_in, wv, ld.at[5]),
    ]
    for copy in local:
        copy.start()
    pl.semaphore_wait(barrier, len(greeted))

    @pl.when(ctx < NCTX - 1)
    def _():
        remote(xin.at[pl.ds(TOK - 16, 16)], halo, halos.at[0], halor.at[0], {"ctx": after}).start()

    right = {"ctx": lax.rem(z + 1, NZ) * 2 + c}
    left = {"ctx": lax.rem(z + NZ - 1, NZ) * 2 + c}

    def rows_of(zb, core, p):
        start = pl.multiple_of((zb * 2 + core) * HB + p * HP, HP)
        return head.at[pl.ds(start, HP)]

    def hop(way, k, p):
        zb = lax.rem(z + NZ - k, NZ) if way == 0 else lax.rem(z + k, NZ)
        where = rows_of(zb, c, p)
        src = head_in.at[pl.ds(p * HP, HP)] if k == 0 else where
        return remote(src, where, hs.at[way, k, p], hr.at[way, k, p], right if way == 0 else left)

    def arrival(way, k, p):
        zb = lax.rem(z + NZ - 1 - k, NZ) if way == 0 else lax.rem(z + 1 + k, NZ)
        where = rows_of(zb, c, p)
        return remote(where, where, hs.at[way, k, p], hr.at[way, k, p], right if way == 0 else left), where

    def valid(way, k, p):
        return k < 3 or (k == 3 and p == way)

    def pump(k, p):
        for way in range(2):
            if valid(way, k, p):
                got_it, where = arrival(way, k, p)
                got_it.wait_recv()
                if valid(way, k + 1, p):
                    begin(hop(way, k + 1, p))
                begin(remote(where, where, hps.at[way, k, p], hpr.at[way, k, p], partner))

    for p in range(2):
        for way in range(2):
            begin(hop(way, 0, p))
    mine_rows = head.at[own]
    begin(remote(head_in, mine_rows, hps.at[0, 3, 1], hpr.at[0, 3, 1], partner))

    for lt in range(8):
        lanes = slice(128 * lt, 128 * lt + 128)
        for h in range(2):
            dflat[pl.ds(lt + 64 * h, 8, stride=8), :] = decay_in[8 * h : 8 * h + 8, lanes]
    local[0].wait()
    for k in range(TOK // 32):
        xpad[8 + 32 * k : 40 + 32 * k, :] = xs[32 * k : 32 * k + 32, :].astype(F32)

    @pl.when(ctx > 0)
    def _():
        remote(xin.at[pl.ds(TOK - 16, 16)], halo, halos.at[0], halor.at[0], {"ctx": after}).wait_recv()
        xpad[0:8, :] = halo[...].astype(F32)[8:16, :]

    @pl.when(ctx == 0)
    def _():
        xpad[0:8, :] = jnp.zeros((8, CH), F32)

    local[1].wait()
    sends1 = {}
    for t in range(NT):
        for k in range(TC // 32):
            r0 = TC * t + 32 * k
            for half in range(2):
                lanes = slice(512 * half, 512 * half + 512)
                v = jnp.zeros((32, 512), F32) + conv_b[:, lanes]
                for offset in range(KCONV):
                    v = v + conv_w[offset : offset + 1, lanes] * xpad[r0 + 5 + offset : r0 + 37 + offset, lanes]
                sm[r0 : r0 + 32, lanes] = sigmoid_linear(v).astype(BF16)
        product = lax.dot_general(
            sel[...], sm[TC * t : TC * t + TC, :], (((1,), (1,)), ((), ())), preferred_element_type=F32
        )
        pb[t] = product[:RANK].astype(BF16)
        bcp[t] = product[RANK:]
        for k, p in enumerate(others):
            rows = pl.ds(pl.multiple_of(p * ROWS, ROWS), ROWS)
            sends1[t, k] = begin(remote(pb.at[t, rows], recv.at[t, k], s1.at[t, k], r1.at[t, k], {"ch": p}))
        for k in range(4):
            @pl.when(ch != 5 * k)
            def _():
                tile(t, k, ch, bcp, recvx, sx, rx).start()

    local[3].wait()
    for k in range(TOK // 32):
        sg[32 * k : 32 * k + 32, :] = sigmoid_linear(gs[32 * k : 32 * k + 32, :].astype(F32))

    myrows = pl.ds(pl.multiple_of(ch * ROWS, ROWS), ROWS)
    sends2 = {}
    for t in range(NT):
        for k in range(NCH - 1):
            sends1[t, k].wait_recv()
        summed = pb[t, myrows].astype(F32)
        for k in range(NCH - 1):
            summed = summed + recv[t, k].astype(F32)
        mine[t] = summed.astype(BF16)
        for k, p in enumerate(others):
            sends2[t, k] = begin(remote(mine.at[t], proj.at[t, myrows], s2.at[t, k], r2.at[t, k], {"ch": p}))
        proj[t, myrows] = mine[t]
        for k in range(4):
            @pl.when(ch == 5 * k)
            def _():
                sumx = bcp[t, 8 * k : 8 * k + 8]
                for j in range(NCH - 1):
                    remote(minex.at[t], recvx.at[t, j], sx.at[t, 0], rx.at[t, j], {"ch": others[0]}).wait_recv()
                    sumx = sumx + recvx[t, j]
                minex[t] = sumx
                for j in range(NCH - 1):
                    remote(
                        minex.at[t], bc.at[t, pl.ds(8 * k, 8)], sy.at[t, j], ry.at[t, k], {"ch": others[j]}
                    ).start()
                bc[t, 8 * k : 8 * k + 8] = minex[t]

    pump(0, 0)

    local[2].wait()
    rates = [-jnp.exp(dflat[8 * n : 8 * n + 8, :]) for n in range(STATE)]
    carry = (jnp.zeros((8, 128), F32),) * (STATE + 1)
    for t in range(NT):
        for k in range(NCH - 1):
            sends2[t, k].wait_recv()
        for k in range(4):
            @pl.when(ch != 5 * k)
            def _():
                remote(minex.at[t], bc.at[t, pl.ds(8 * k, 8)], sy.at[t, 0], ry.at[t, k], {"ch": 5 * k}).wait_recv()

        turned = jnp.transpose(bc[t])
        for n in range(2 * STATE):
            bb[n, TC * t : TC * t + TC, :] = jnp.broadcast_to(turned[:, n : n + 1], (TC, 128))
        raw = lax.dot_general(proj[t], stepw[...], (((0,), (0,)), ((), ())), preferred_element_type=F32)
        v = raw + step_b[...]
        dt = jnp.maximum(v, 0.0) + jnp.log1p(jnp.exp(-jnp.abs(v)))
        u = dt * sm[TC * t : TC * t + TC, :].astype(F32)
        for b in range(TC // 8):
            for lt in range(8):
                start = (TC // 8 * t + b) * 64 + lt * 8
                dtf[start : start + 8, :] = dt[8 * b : 8 * b + 8, 128 * lt : 128 * lt + 128]
                uf[start : start + 8, :] = u[8 * b : 8 * b + 8, 128 * lt : 128 * lt + 128]

        def step(tb, held):
            s, elapsed = list(held[:STATE]), held[STATE]
            for r in range(8):
                rows = pl.ds(tb * 64 + r, 8, stride=8)
                dt = dtf[rows, :]
                u = uf[rows, :]
                splat = pl.ds(tb * 8 + r, 8, stride=0)
                y = None
                for n in range(STATE):
                    s[n] = jnp.exp(dt * rates[n]) * s[n] + u * bb[n, splat, :]
                    term = s[n] * bb[STATE + n, splat, :]
                    y = term if y is None else y + term
                elapsed = elapsed + dt
                uf[rows, :] = y
                dtf[rows, :] = elapsed
            return (*s, elapsed)

        carry = lax.fori_loop(TC // 8 * t, TC // 8 * (t + 1), step, carry)
        if t == 1:
            pump(0, 1)
    for n in range(STATE):
        state[8 * n : 8 * n + 8, :] = carry[n]
    total[...] = carry[STATE]

    half = pl.ds(pl.multiple_of(c * HALF, HALF), HALF)
    other = pl.ds(pl.multiple_of((1 - c) * HALF, HALF), HALF)
    swap_s[...] = state[other, :]
    a = begin(remote(swap_s, got_s, cs.at[0], cr.at[0], partner))
    b = begin(remote(total, got_e, cs.at[1], cr.at[1], partner))
    rate = -jnp.exp(dflat[half, :])

    def through(elapsed):
        return jnp.exp(rate * jnp.tile(elapsed, (HALF // 8, 1)))

    a.wait_recv()
    b.wait_recv()
    own_s, own_e, oth_s, oth_e = state[half, :], total[...], got_s[...], got_e[...]
    low = c == 0
    t0, t1 = jnp.where(low, own_s, oth_s), jnp.where(low, oth_s, own_s)
    e0, e1 = jnp.where(low, own_e, oth_e), jnp.where(low, oth_e, own_e)
    send_s[...] = (through(e1) * t0 + t1).astype(send_s.dtype)
    send_e[...] = e0 + e1

    def pair(d, sign):
        peer = {"ctx": (z + sign * d) * 2 + c}
        return (
            remote(send_s, zs.at[d - 1], csz.at[0, d - 1], crz.at[0, d - 1], peer),
            remote(send_e, ze.at[d - 1], csz.at[1, d - 1], crz.at[1, d - 1], peer),
        )

    for d in range(1, NZ):
        @pl.when(z + d < NZ)
        def _():
            for copy in pair(d, 1):
                copy.start()

    pump(1, 0)
    hold[...] = jnp.zeros_like(hold)
    for d in range(NZ - 1, 0, -1):
        @pl.when(z >= d)
        def _():
            for copy in pair(d, -1):
                copy.wait_recv()
            hold[...] = through(ze[d - 1]) * hold[...] + zs[d - 1].astype(F32)

    into0 = hold[...]
    into1 = through(e0) * into0 + t0
    fin[...] = jnp.where(low, into1, into0)
    into[half, :] = jnp.where(low, into0, into1)
    f = begin(remote(fin, into.at[half], csf.at[0], crf.at[0], partner))
    f.wait_recv()

    came = [into[8 * n : 8 * n + 8, :] for n in range(STATE)]

    def fix(tb, _):
        for r in range(8):
            rows = pl.ds(tb * 64 + r, 8, stride=8)
            elapsed = dtf[rows, :]
            y = uf[rows, :]
            splat = pl.ds(tb * 8 + r, 8, stride=0)
            for n in range(STATE):
                y = y + jnp.exp(elapsed * rates[n]) * came[n] * bb[STATE + n, splat, :]
            uf[rows, :] = y
        return 0

    lax.fori_loop(0, NTB, fix, 0)
    for k in range(TOK // 16):
        rows = slice(16 * k, 16 * k + 16)
        for lt in range(8):
            lanes = slice(128 * lt, 128 * lt + 128)
            start = (2 * k) * 64 + lt * 8
            scanned = jnp.concatenate([uf[start : start + 8, :], uf[start + 64 : start + 72, :]], axis=0)
            value = scanned + skip[:, lanes] * sm[rows, lanes].astype(F32)
            mixer[rows, lanes] = (value * sg[rows, lanes]).astype(BF16)
    pump(1, 1)

    bits = cube_of(ch)

    def block(r):
        return index_of([lax.rem(bits[d] + ((r >> d) & 1), 2) for d in range(4)])

    def lanes_of(r):
        return pl.ds(pl.multiple_of(block(r) * BLK, BLK), BLK)

    peers = [{"ch": block(1 << d)} for d in range(4)]

    def rows(q):
        return pl.ds(QR * q, QR)

    def dim(q, s):
        return (q + s) % 4

    def kept(q, s):
        return [r for r in range(16) if all(not (r >> dim(q, i)) & 1 for i in range(s))]

    def slot(q, s, r):
        return SLOT[s] + kept(q, s + 1).index(r)

    def send(q, s, r):
        d = dim(q, s)
        k = slot(q, s, r ^ (1 << d))
        begin(remote(part.at[r, rows(q)], got.at[k, rows(q)], ms.at[r, q], mr.at[k, q], peers[d]))

    def take(q, s, r):
        k = slot(q, s, r)
        remote(part.at[r, rows(q)], got.at[k, rows(q)], ms.at[r, q], mr.at[k, q], peers[dim(q, s)]).wait_recv()
        return got[k, rows(q)].astype(F32)

    local[5].wait()
    for r in [15, 14, 13, 11, 7, 12, 10, 9, 6, 5, 3, 8, 4, 2, 1, 0]:
        product = jnp.dot(mixer[...], wv[:, lanes_of(r)], preferred_element_type=F32)
        acc[r] = product
        part[r] = product.astype(BF16)
        for q in range(NQ):
            if (r >> dim(q, 0)) & 1:
                send(q, 0, r)
    pump(2, 0)
    for s in range(3):
        for q in range(NQ):
            left_over = kept(q, s + 1)
            d = dim(q, s + 1)
            for r in [r for r in left_over if (r >> d) & 1] + [r for r in left_over if not (r >> d) & 1]:
                value = acc[r, rows(q)] + take(q, s, r)
                if (r >> d) & 1:
                    part[r, rows(q)] = value.astype(BF16)
                    send(q, s + 1, r)
                else:
                    acc[r, rows(q)] = value
        if s == 1:
            pump(2, 1)

    def give(q, s, r):
        d = dim(q, s)
        where = scaled.at[rows(q), lanes_of(r)]
        begin(remote(where, where, gsn.at[q, s, r], grv.at[q, s, r ^ (1 << d)], peers[d]))

    def spread(q, s):
        held = [0]
        for i in range(s):
            held = held + [r ^ (1 << dim(q, i)) for r in held]
        return held

    for q in range(NQ):
        hidden = residual[rows(q), :].astype(F32) + (acc[0, rows(q)] + take(q, 3, 0))
        scaled[rows(q), lanes_of(0)] = (hidden * gain[:, lanes_of(0)]).astype(BF16)
        give(q, 0, 0)
    for s in range(4):
        for q in range(NQ):
            for r in spread(q, s):
                r = r ^ (1 << dim(q, s))
                where = scaled.at[rows(q), lanes_of(r)]
                remote(where, where, gsn.at[q, s, r], grv.at[q, s, r], peers[dim(q, s)]).wait_recv()
            if s < 3:
                for r in spread(q, s + 1):
                    give(q, s + 1, r)
        if s == 1:
            for p in range(2):
                pump(3, p)

    local[4].wait()
    for k in range(4):
        for p in range(2):
            for way in range(2):
                if valid(way, k, p):
                    where = head.at[pl.ds(0, HP)]
                    remote(where, where, hps.at[way, k, p], hpr.at[way, k, p], partner).wait_recv()
    remote(head_in, mine_rows, hps.at[0, 3, 1], hpr.at[0, 3, 1], partner).wait_recv()

    def square(k, held):
        where = pl.ds(pl.multiple_of(k * BLK, BLK), BLK)
        h = scaled[:, where].astype(F32) / gain[:, where]
        acc[8] += h * h
        return held

    acc[8] = jnp.zeros((TOK, BLK), F32)
    lax.fori_loop(0, NCH, square, 0)
    rms[...] = lax.rsqrt(jnp.sum(acc[8], axis=1, keepdims=True) * (1.0 / D) + 1e-06)

    def logit(j, held):
        where = pl.ds(pl.multiple_of(j * VT, VT), VT)
        acc[j] = jnp.dot(scaled[...], head[:, where], preferred_element_type=F32) * rms[...]
        return held

    lax.fori_loop(0, NVT, logit, 0)
    tcol[...] = jnp.transpose(jnp.broadcast_to((targets[...] - ch * VOC).astype(F32), (128, TOK)))
    lane = lax.broadcasted_iota(jnp.int32, (32, VT), 1).astype(F32)
    place = lax.broadcasted_iota(jnp.int32, (32, 128), 1)

    def tally(k, held):
        here = pl.ds(pl.multiple_of(k * 32, 32), 32)
        values = [acc[j, here] for j in range(NVT)]
        peak = values[0]
        for v in values[1:]:
            peak = jnp.maximum(peak, v)
        peak = jnp.max(peak, axis=1, keepdims=True)
        want = tcol[here, :][:, 0:1]
        sums = [jnp.zeros((32, VT), F32) for _ in range(4)]
        for j, v in enumerate(values):
            shifted = v - peak
            w = jnp.exp(shifted)
            ws = w * shifted
            sums[0] = sums[0] + w
            sums[1] = sums[1] + ws
            sums[2] = sums[2] + ws * shifted
            sums[3] = sums[3] + jnp.where(lane + float(j * VT) == want, v, 0.0)
        cols = [peak] + [jnp.sum(v, axis=1, keepdims=True) for v in sums]
        packed = jnp.zeros((32, 128), F32)
        for i, v in enumerate(cols):
            packed = jnp.where(place == i, v, packed)
        tcol[here, :] = packed
        return held

    lax.fori_loop(0, TOK // 32, tally, 0)

    stat[...] = jnp.transpose(tcol[...])[:8, :]
    sends3 = [begin(remote(stat, gstat.at[k], es.at[k], er.at[k], {"ch": p})) for k, p in enumerate(others)]
    for copy in sends3:
        copy.wait_recv()
    parts = [stat[...]] + [gstat[k] for k in range(NCH - 1)]
    peak = parts[0][0:1, :]
    for v in parts[1:]:
        peak = jnp.maximum(peak, v[0:1, :])
    sum0 = sum1 = sum2 = picked = jnp.zeros((1, TOK), F32)
    for v in parts:
        d = v[0:1, :] - peak
        w = jnp.exp(d)
        wd = w * d
        sum0 = sum0 + w * v[1:2, :]
        sum1 = sum1 + (w * v[2:3, :] + wd * v[1:2, :])
        sum2 = sum2 + (w * v[3:4, :] + 2.0 * wd * v[2:3, :] + wd * d * v[1:2, :])
        picked = picked + v[4:5, :]
    log_total = jnp.log(sum0)
    ratio = sum1 / sum0
    out[0:1, :] = picked - peak - log_total
    out[1:2, :] = ratio - log_total
    out[2:3, :] = sum2 / sum0 - ratio * ratio
    out[3:8, :] = jnp.zeros((5, TOK), F32)

    for copy in pending:
        copy.wait_send()

    @pl.when(ctx < NCTX - 1)
    def _():
        remote(xin.at[pl.ds(TOK - 16, 16)], halo, halos.at[0], halor.at[0], {"ctx": after}).wait_send()

    for d in range(1, NZ):
        @pl.when(z + d < NZ)
        def _():
            for copy in pair(d, 1):
                copy.wait_send()
    for t in range(NT):
        for k in range(4):
            @pl.when(ch != 5 * k)
            def _():
                tile(t, k, ch, bcp, recvx, sx, rx).wait_send()

            @pl.when(ch == 5 * k)
            def _():
                for j in range(NCH - 1):
                    remote(
                        minex.at[t], bc.at[t, pl.ds(8 * k, 8)], sy.at[t, j], ry.at[t, k], {"ch": others[j]}
                    ).wait_send()


def tile(t, k, ch, bcp, recvx, sx, rx):
    where = lax.rem(ch - 5 * k + 2 * NCH, NCH) - 1
    return remote(bcp.at[t, pl.ds(8 * k, 8)], recvx.at[t, where], sx.at[t, k], rx.at[t, where], {"ch": 5 * k})


def per_device(
    layer_input, gate_input, conv_weight, conv_bias, select_weight, step_weight, step_bias, decay_log,
    skip_gain, out_weight, residual, norm_gain, head_weight, targets,
):
    n = NCH - 1
    dma = pltpu.SemaphoreType.DMA
    v = pltpu.VMEM
    result = pl.pallas_call(
        kernel,
        out_shape=jax.ShapeDtypeStruct((8, TOK), F32),
        in_specs=[HBM] * 6 + [VM] * 8,
        out_specs=VM,
        scratch_shapes=[
            v((TOK, CH), BF16), v((TOK, CH), BF16), v((RANK + 2 * STATE, CH), BF16), v((RANK, CH), BF16),
            v((CH, D), BF16), v((D, VOC), BF16), v((16, CH), BF16), v((TOK + 8, CH), F32), v((TOK, CH), BF16),
            v((TOK, CH), F32), v((STATE * 8, 128), F32),
            v((NT, RANK, TC), BF16), v((NT, 2 * STATE, TC), F32), v((NT, n, ROWS, TC), BF16), v((NT, ROWS, TC), BF16),
            v((NT, RANK, TC), BF16), v((NT, n, 8, TC), F32), v((NT, 8, TC), F32), v((NT, 2 * STATE, TC), F32),
            v((2 * STATE, TOK, 128), F32),
            v((FLAT, 128), F32), v((FLAT, 128), F32), v((STATE * 8, 128), F32), v((8, 128), F32),
            v((HALF, 128), F32), v((HALF, 128), F32), v((8, 128), F32),
            v((HALF, 128), BF16), v((8, 128), F32), v((NZ - 1, HALF, 128), BF16), v((NZ - 1, 8, 128), F32),
            v((HALF, 128), F32), v((HALF, 128), F32), v((STATE * 8, 128), F32),
            v((TOK, CH), BF16), v((NCH, TOK, BLK), F32), v((NCH, TOK, BLK), BF16), v((15, TOK, BLK), BF16),
            v((TOK, D), BF16), v((TOK, 1), F32), v((TOK, 128), F32), v((8, TOK), F32), v((n, 8, TOK), F32),
            dma((6,)), dma((2, 4, 2)), dma((2, 4, 2)), dma((2, 4, 2)), dma((2, 4, 2)), dma((1,)), dma((1,)),
            dma((NT, n)), dma((NT, n)), dma((NT, n)), dma((NT, n)),
            dma((NT, 4)), dma((NT, n)), dma((NT, n)), dma((NT, 4)),
            dma((2,)), dma((2,)), dma((2, NZ - 1)), dma((2, NZ - 1)), dma((1,)), dma((1,)),
            dma((NCH, NQ)), dma((15, NQ)), dma((NQ, 4, NCH)), dma((NQ, 4, NCH)), dma((n,)), dma((n,)),
        ],
        compiler_params=pltpu.CompilerParams(
            vmem_limit_bytes=67043328, collective_id=0, has_side_effects=True
        ),
        name="score_window",
    )(
        layer_input, gate_input, select_weight, step_weight, out_weight, head_weight, residual, conv_weight,
        conv_bias[None, :], step_bias[None, :], decay_log, skip_gain[None, :], norm_gain[None, :], targets[None, :],
    )
    return result[0], result[1], result[2]


def solution(mesh):
    in_specs = (
        P("ctx", "ch"), P("ctx", "ch"), P(None, "ch"), P("ch"), P(None, "ch"), P(None, "ch"), P("ch"),
        P(None, "ch"), P("ch"), P("ch", None), P("ctx", "ch"), P(), P("ctx", "ch"), P("ctx"),
    )
    return jax.shard_map(
        per_device, mesh=mesh, in_specs=in_specs, out_specs=(P("ctx"), P("ctx"), P("ctx")), check_vma=False
    )
```

```python
import jax
import jax.numpy as jnp
from jax import lax
from jax.experimental import pallas as pl
from jax.experimental.pallas import tpu as pltpu
from jax.sharding import PartitionSpec as P

STATE = 16
RANK = 512
KCONV = 4
TOK = 384
CH = 1024
D = 4096
VOC = 2048
NCH = 16
NCTX = 16
NZ = 8
NT = 3
TC = TOK // NT
ROWS = RANK // NCH
NTB = TOK // 8
FLAT = NTB * 64
HALF = STATE * 4
NK = 2
TK = TOK // NK
NQ = 4 * NK
QR = TOK // NQ
BLK = D // NCH
HB = D // NCTX
HP = HB // 2
VT = 256
NVT = VOC // VT
MESH = pl.DeviceIdType.MESH
F32 = jnp.float32
BF16 = jnp.bfloat16
VM = pl.BlockSpec(memory_space=pltpu.VMEM)
HBM = pl.BlockSpec(memory_space=pl.ANY)
SLOT = (0, 8, 12, 14)


def remote(src, dst, send_sem, recv_sem, peer):
    return pltpu.make_async_remote_copy(
        src_ref=src, dst_ref=dst, send_sem=send_sem, recv_sem=recv_sem, device_id=peer, device_id_type=MESH
    )


def sigmoid_linear(operand):
    return operand / (1.0 + jnp.exp(-operand))


def cube_of(index):
    x, y = index // 4, lax.rem(index, 4)
    return [lax.rem(x + x // 2, 2), x // 2, lax.rem(y + y // 2, 2), y // 2]


def index_of(bits):
    def line(low, high):
        return high * 2 + lax.rem(high + low, 2)

    return line(bits[0], bits[1]) * 4 + line(bits[2], bits[3])


def kernel(
    xin, gate_in, select_in, stepw_in, outw_in, head_in, residual, conv_w, conv_b, step_b, decay_in, skip, gain, targets,
    out,
    xs, gs, sel, stepw, wv, head, halo, xpad, sm, sg, dflat, pb, bcp, recv, mine, proj, recvx, minex, bc, bb,
    dtf, uf, state, total, swap_s, got_s, got_e, send_s, send_e, zs, ze, hold, fin, into,
    mixer, acc, part, got, scaled, rms, tcol, stat, gstat,
    ld, hs, hr, hps, hpr, halos, halor, s1, r1, s2, r2, sx, rx, sy, ry, cs, cr, csz, crz, csf, crf, ms, mr, gsn, grv, es, er,
):
    ch = lax.axis_index("ch")
    ctx = lax.axis_index("ctx")
    z, c = ctx // 2, lax.rem(ctx, 2)
    pending = []

    def begin(copy):
        copy.start()
        pending.append(copy)
        return copy

    others = [lax.rem(ch + off, NCH) for off in range(1, NCH)]
    partner = {"ctx": z * 2 + 1 - c}
    after, before = lax.rem(ctx + 1, NCTX), lax.rem(ctx + NCTX - 1, NCTX)
    cross = jnp.where(c == 0, before, after)
    greeted = [{"ch": p} for p in others] + [partner, {"ctx": cross}]
    greeted += [{"ctx": lax.rem(z + d, NZ) * 2 + c} for d in range(1, NZ)]
    barrier = pltpu.get_barrier_semaphore()
    for peer in greeted:
        pl.semaphore_signal(barrier, inc=1, device_id=peer, device_id_type=MESH)

    own = pl.ds(pl.multiple_of(ctx * HB, HB), HB)
    local = [
        pltpu.make_async_copy(xin, xs, ld.at[0]),
        pltpu.make_async_copy(select_in, sel, ld.at[1]),
        pltpu.make_async_copy(stepw_in, stepw, ld.at[2]),
        pltpu.make_async_copy(gate_in, gs, ld.at[3]),
        pltpu.make_async_copy(head_in, head.at[own], ld.at[4]),
        pltpu.make_async_copy(outw_in, wv, ld.at[5]),
    ]
    for copy in local:
        copy.start()
    pl.semaphore_wait(barrier, len(greeted))

    @pl.when(ctx < NCTX - 1)
    def _():
        remote(xin.at[pl.ds(TOK - 16, 16)], halo, halos.at[0], halor.at[0], {"ctx": after}).start()

    right = {"ctx": lax.rem(z + 1, NZ) * 2 + c}
    left = {"ctx": lax.rem(z + NZ - 1, NZ) * 2 + c}

    def rows_of(zb, core, p):
        start = pl.multiple_of((zb * 2 + core) * HB + p * HP, HP)
        return head.at[pl.ds(start, HP)]

    def hop(way, k, p):
        zb = lax.rem(z + NZ - k, NZ) if way == 0 else lax.rem(z + k, NZ)
        where = rows_of(zb, c, p)
        src = head_in.at[pl.ds(p * HP, HP)] if k == 0 else where
        return remote(src, where, hs.at[way, k, p], hr.at[way, k, p], right if way == 0 else left)

    def arrival(way, k, p):
        zb = lax.rem(z + NZ - 1 - k, NZ) if way == 0 else lax.rem(z + 1 + k, NZ)
        where = rows_of(zb, c, p)
        return remote(where, where, hs.at[way, k, p], hr.at[way, k, p], right if way == 0 else left), where

    def valid(way, k, p):
        return k < 3 or (k == 3 and p == way)

    def relay(k, p):
        for way in range(2):
            if valid(way, k, p):
                arrival(way, k, p)[0].wait_recv()
                if valid(way, k + 1, p):
                    begin(hop(way, k + 1, p))

    def share(k, p):
        for way in range(2):
            if valid(way, k, p):
                where = arrival(way, k, p)[1]
                begin(remote(where, where, hps.at[way, k, p], hpr.at[way, k, p], partner))

    def pump(k, p):
        relay(k, p)
        share(k, p)

    for p in range(2):
        for way in range(2):
            begin(hop(way, 0, p))
    mine_rows = head.at[own]
    begin(remote(head_in, mine_rows, hps.at[0, 3, 1], hpr.at[0, 3, 1], partner))

    for lt in range(8):
        lanes = slice(128 * lt, 128 * lt + 128)
        for h in range(2):
            dflat[pl.ds(lt + 64 * h, 8, stride=8), :] = decay_in[8 * h : 8 * h + 8, lanes]
    local[0].wait()
    for k in range(TOK // 32):
        xpad[8 + 32 * k : 40 + 32 * k, :] = xs[32 * k : 32 * k + 32, :].astype(F32)

    @pl.when(ctx > 0)
    def _():
        remote(xin.at[pl.ds(TOK - 16, 16)], halo, halos.at[0], halor.at[0], {"ctx": after}).wait_recv()
        xpad[0:8, :] = halo[...].astype(F32)[8:16, :]

    @pl.when(ctx == 0)
    def _():
        xpad[0:8, :] = jnp.zeros((8, CH), F32)

    local[1].wait()
    sends1 = {}
    for t in range(NT):
        for k in range(TC // 32):
            r0 = TC * t + 32 * k
            for half in range(2):
                lanes = slice(512 * half, 512 * half + 512)
                v = jnp.zeros((32, 512), F32) + conv_b[:, lanes]
                for offset in range(KCONV):
                    v = v + conv_w[offset : offset + 1, lanes] * xpad[r0 + 5 + offset : r0 + 37 + offset, lanes]
                sm[r0 : r0 + 32, lanes] = sigmoid_linear(v).astype(BF16)
        product = lax.dot_general(
            sel[...], sm[TC * t : TC * t + TC, :], (((1,), (1,)), ((), ())), preferred_element_type=F32
        )
        pb[t] = product[:RANK].astype(BF16)
        bcp[t] = product[RANK:]
        for k, p in enumerate(others):
            rows = pl.ds(pl.multiple_of(p * ROWS, ROWS), ROWS)
            sends1[t, k] = begin(remote(pb.at[t, rows], recv.at[t, k], s1.at[t, k], r1.at[t, k], {"ch": p}))
        for k in range(4):
            @pl.when(ch != 5 * k)
            def _():
                tile(t, k, ch, bcp, recvx, sx, rx).start()

    local[3].wait()
    for k in range(TOK // 32):
        sg[32 * k : 32 * k + 32, :] = sigmoid_linear(gs[32 * k : 32 * k + 32, :].astype(F32))

    myrows = pl.ds(pl.multiple_of(ch * ROWS, ROWS), ROWS)
    sends2 = {}
    for t in range(NT):
        for k in range(NCH - 1):
            sends1[t, k].wait_recv()
        summed = pb[t, myrows].astype(F32)
        for k in range(NCH - 1):
            summed = summed + recv[t, k].astype(F32)
        mine[t] = summed.astype(BF16)
        for k, p in enumerate(others):
            sends2[t, k] = begin(remote(mine.at[t], proj.at[t, myrows], s2.at[t, k], r2.at[t, k], {"ch": p}))
        proj[t, myrows] = mine[t]
        for k in range(4):
            @pl.when(ch == 5 * k)
            def _():
                sumx = bcp[t, 8 * k : 8 * k + 8]
                for j in range(NCH - 1):
                    remote(minex.at[t], recvx.at[t, j], sx.at[t, 0], rx.at[t, j], {"ch": others[0]}).wait_recv()
                    sumx = sumx + recvx[t, j]
                minex[t] = sumx
                for j in range(NCH - 1):
                    remote(
                        minex.at[t], bc.at[t, pl.ds(8 * k, 8)], sy.at[t, j], ry.at[t, k], {"ch": others[j]}
                    ).start()
                bc[t, 8 * k : 8 * k + 8] = minex[t]

    pump(0, 0)

    local[2].wait()
    rates = [-jnp.exp(dflat[8 * n : 8 * n + 8, :]) for n in range(STATE)]
    carry = (jnp.zeros((8, 128), F32),) * (STATE + 1)
    for t in range(NT):
        for k in range(NCH - 1):
            sends2[t, k].wait_recv()
        for k in range(4):
            @pl.when(ch != 5 * k)
            def _():
                remote(minex.at[t], bc.at[t, pl.ds(8 * k, 8)], sy.at[t, 0], ry.at[t, k], {"ch": 5 * k}).wait_recv()

        turned = jnp.transpose(bc[t])
        for n in range(2 * STATE):
            bb[n, TC * t : TC * t + TC, :] = jnp.broadcast_to(turned[:, n : n + 1], (TC, 128))
        raw = lax.dot_general(proj[t], stepw[...], (((0,), (0,)), ((), ())), preferred_element_type=F32)
        v = raw + step_b[...]
        dt = jnp.maximum(v, 0.0) + jnp.log1p(jnp.exp(-jnp.abs(v)))
        u = dt * sm[TC * t : TC * t + TC, :].astype(F32)
        for b in range(TC // 8):
            for lt in range(8):
                start = (TC // 8 * t + b) * 64 + lt * 8
                dtf[start : start + 8, :] = dt[8 * b : 8 * b + 8, 128 * lt : 128 * lt + 128]
                uf[start : start + 8, :] = u[8 * b : 8 * b + 8, 128 * lt : 128 * lt + 128]

        def step(tb, held):
            s, elapsed = list(held[:STATE]), held[STATE]
            for r in range(8):
                rows = pl.ds(tb * 64 + r, 8, stride=8)
                dt = dtf[rows, :]
                u = uf[rows, :]
                splat = pl.ds(tb * 8 + r, 8, stride=0)
                y = None
                for n in range(STATE):
                    s[n] = jnp.exp(dt * rates[n]) * s[n] + u * bb[n, splat, :]
                    term = s[n] * bb[STATE + n, splat, :]
                    y = term if y is None else y + term
                elapsed = elapsed + dt
                uf[rows, :] = y
                dtf[rows, :] = elapsed
            return (*s, elapsed)

        carry = lax.fori_loop(TC // 8 * t, TC // 8 * (t + 1), step, carry)
    for n in range(STATE):
        state[8 * n : 8 * n + 8, :] = carry[n]
    total[...] = carry[STATE]

    half = pl.ds(pl.multiple_of(c * HALF, HALF), HALF)
    other = pl.ds(pl.multiple_of((1 - c) * HALF, HALF), HALF)
    swap_s[...] = state[other, :]
    a = begin(remote(swap_s, got_s, cs.at[0], cr.at[0], partner))
    b = begin(remote(total, got_e, cs.at[1], cr.at[1], partner))
    rate = -jnp.exp(dflat[half, :])

    def through(elapsed):
        return jnp.exp(rate * jnp.tile(elapsed, (HALF // 8, 1)))

    a.wait_recv()
    b.wait_recv()
    own_s, own_e, oth_s, oth_e = state[half, :], total[...], got_s[...], got_e[...]
    low = c == 0
    t0, t1 = jnp.where(low, own_s, oth_s), jnp.where(low, oth_s, own_s)
    e0, e1 = jnp.where(low, own_e, oth_e), jnp.where(low, oth_e, own_e)
    send_s[...] = (through(e1) * t0 + t1).astype(send_s.dtype)
    send_e[...] = e0 + e1

    def pair(d, sign):
        peer = {"ctx": (z + sign * d) * 2 + c}
        return (
            remote(send_s, zs.at[d - 1], csz.at[0, d - 1], crz.at[0, d - 1], peer),
            remote(send_e, ze.at[d - 1], csz.at[1, d - 1], crz.at[1, d - 1], peer),
        )

    for d in range(1, NZ):
        @pl.when(z + d < NZ)
        def _():
            for copy in pair(d, 1):
                copy.start()

    relay(0, 1)
    hold[...] = jnp.zeros_like(hold)
    for d in range(NZ - 1, 0, -1):
        @pl.when(z >= d)
        def _():
            for copy in pair(d, -1):
                copy.wait_recv()
            hold[...] = through(ze[d - 1]) * hold[...] + zs[d - 1].astype(F32)

    into0 = hold[...]
    into1 = through(e0) * into0 + t0
    fin[...] = jnp.where(low, into1, into0)
    into[half, :] = jnp.where(low, into0, into1)
    f = begin(remote(fin, into.at[half], csf.at[0], crf.at[0], partner))
    f.wait_recv()
    relay(1, 0)
    share(0, 1)
    share(1, 0)

    came = [into[8 * n : 8 * n + 8, :] for n in range(STATE)]

    def fix(tb, _):
        for r in range(8):
            rows = pl.ds(tb * 64 + r, 8, stride=8)
            elapsed = dtf[rows, :]
            y = uf[rows, :]
            splat = pl.ds(tb * 8 + r, 8, stride=0)
            for n in range(STATE):
                y = y + jnp.exp(elapsed * rates[n]) * came[n] * bb[STATE + n, splat, :]
            uf[rows, :] = y
        return 0

    def gate_chunk(ck):
        lax.fori_loop(NTB // NK * ck, NTB // NK * (ck + 1), fix, 0)
        for k in range(TK // 16 * ck, TK // 16 * (ck + 1)):
            rows = slice(16 * k, 16 * k + 16)
            for lt in range(8):
                lanes = slice(128 * lt, 128 * lt + 128)
                start = (2 * k) * 64 + lt * 8
                scanned = jnp.concatenate([uf[start : start + 8, :], uf[start + 64 : start + 72, :]], axis=0)
                value = scanned + skip[:, lanes] * sm[rows, lanes].astype(F32)
                mixer[rows, lanes] = (value * sg[rows, lanes]).astype(BF16)

    bits = cube_of(ch)

    def block(r):
        return index_of([lax.rem(bits[d] + ((r >> d) & 1), 2) for d in range(4)])

    def lanes_of(r):
        return pl.ds(pl.multiple_of(block(r) * BLK, BLK), BLK)

    peers = [{"ch": block(1 << d)} for d in range(4)]

    def rows(q):
        return pl.ds(QR * q, QR)

    def dim(q, s):
        return (q + s) % 4

    def kept(q, s):
        return [r for r in range(16) if all(not (r >> dim(q, i)) & 1 for i in range(s))]

    def slot(q, s, r):
        return SLOT[s] + kept(q, s + 1).index(r)

    def send(q, s, r):
        d = dim(q, s)
        k = slot(q, s, r ^ (1 << d))
        begin(remote(part.at[r, rows(q)], got.at[k, rows(q)], ms.at[r, q], mr.at[k, q], peers[d]))

    def take(q, s, r):
        k = slot(q, s, r)
        remote(part.at[r, rows(q)], got.at[k, rows(q)], ms.at[r, q], mr.at[k, q], peers[dim(q, s)]).wait_recv()
        return got[k, rows(q)].astype(F32)

    def groups(ck):
        return range(4 * ck, 4 * ck + 4)

    def multiply(ck):
        here = slice(TK * ck, TK * ck + TK)
        for r in [15, 14, 13, 11, 7, 12, 10, 9, 6, 5, 3, 8, 4, 2, 1, 0]:
            product = jnp.dot(mixer[here, :], wv[:, lanes_of(r)], preferred_element_type=F32)
            acc[r, here] = product
            part[r, here] = product.astype(BF16)
            for q in groups(ck):
                if (r >> dim(q, 0)) & 1:
                    send(q, 0, r)

    def fold(ck, s):
        for q in groups(ck):
            left_over = kept(q, s + 1)
            d = dim(q, s + 1)
            for r in [r for r in left_over if (r >> d) & 1] + [r for r in left_over if not (r >> d) & 1]:
                value = acc[r, rows(q)] + take(q, s, r)
                if (r >> d) & 1:
                    part[r, rows(q)] = value.astype(BF16)
                    send(q, s + 1, r)
                else:
                    acc[r, rows(q)] = value

    def spread(q, s):
        held = [0]
        for i in range(s):
            held = held + [r ^ (1 << dim(q, i)) for r in held]
        return held

    def give(q, s, r):
        k = (1 << s) - 1 + spread(q, s).index(r)
        where = scaled.at[rows(q), lanes_of(r)]
        begin(remote(where, where, gsn.at[q, k], grv.at[q, k], peers[dim(q, s)]))

    def finish(ck):
        for q in groups(ck):
            hidden = residual[rows(q), :].astype(F32) + (acc[0, rows(q)] + take(q, 3, 0))
            scaled[rows(q), lanes_of(0)] = (hidden * gain[:, lanes_of(0)]).astype(BF16)
            give(q, 0, 0)

    def widen(ck, s):
        for q in groups(ck):
            for r in spread(q, s):
                k = (1 << s) - 1 + spread(q, s).index(r)
                where = scaled.at[rows(q), lanes_of(r ^ (1 << dim(q, s)))]
                remote(where, where, gsn.at[q, k], grv.at[q, k], peers[dim(q, s)]).wait_recv()
            if s < 3:
                for r in spread(q, s + 1):
                    give(q, s + 1, r)

    def logits(ck):
        here = slice(TK * ck, TK * ck + TK)

        def square(k, held):
            where = pl.ds(pl.multiple_of(k * BLK, BLK), BLK)
            h = scaled[here, where].astype(F32) / gain[:, where]
            acc[8, here] += h * h
            return held

        acc[8, here] = jnp.zeros((TK, BLK), F32)
        lax.fori_loop(0, NCH, square, 0)
        rms[here, :] = lax.rsqrt(jnp.sum(acc[8, here], axis=1, keepdims=True) * (1.0 / D) + 1e-06)

        def logit(j, held):
            where = pl.ds(pl.multiple_of(j * VT, VT), VT)
            acc[j, here] = jnp.dot(scaled[here, :], head[:, where], preferred_element_type=F32) * rms[here, :]
            return held

        lax.fori_loop(0, NVT, logit, 0)

    gate_chunk(0)
    local[5].wait()
    multiply(0)
    gate_chunk(1)
    pump(1, 1)
    fold(0, 0)
    multiply(1)
    fold(0, 1)
    fold(1, 0)
    pump(2, 0)
    fold(0, 2)
    fold(1, 1)
    finish(0)
    fold(1, 2)
    pump(2, 1)
    widen(0, 0)
    finish(1)
    widen(0, 1)
    widen(1, 0)
    widen(0, 2)
    widen(1, 1)
    widen(1, 2)
    widen(0, 3)
    for p in range(2):
        pump(3, p)

    local[4].wait()
    for k in range(4):
        for p in range(2):
            for way in range(2):
                if valid(way, k, p):
                    where = head.at[pl.ds(0, HP)]
                    remote(where, where, hps.at[way, k, p], hpr.at[way, k, p], partner).wait_recv()
    remote(head_in, mine_rows, hps.at[0, 3, 1], hpr.at[0, 3, 1], partner).wait_recv()

    logits(0)
    widen(1, 3)
    logits(1)
    tcol[...] = jnp.transpose(jnp.broadcast_to((targets[...] - ch * VOC).astype(F32), (128, TOK)))
    lane = lax.broadcasted_iota(jnp.int32, (32, VT), 1).astype(F32)
    place = lax.broadcasted_iota(jnp.int32, (32, 128), 1)

    def tally(k, held):
        here = pl.ds(pl.multiple_of(k * 32, 32), 32)
        values = [acc[j, here] for j in range(NVT)]
        peak = values[0]
        for v in values[1:]:
            peak = jnp.maximum(peak, v)
        peak = jnp.max(peak, axis=1, keepdims=True)
        want = tcol[here, :][:, 0:1]
        sums = [jnp.zeros((32, VT), F32) for _ in range(4)]
        for j, v in enumerate(values):
            shifted = v - peak
            w = jnp.exp(shifted)
            ws = w * shifted
            sums[0] = sums[0] + w
            sums[1] = sums[1] + ws
            sums[2] = sums[2] + ws * shifted
            sums[3] = sums[3] + jnp.where(lane + float(j * VT) == want, v, 0.0)
        cols = [peak] + [jnp.sum(v, axis=1, keepdims=True) for v in sums]
        packed = jnp.zeros((32, 128), F32)
        for i, v in enumerate(cols):
            packed = jnp.where(place == i, v, packed)
        tcol[here, :] = packed
        return held

    lax.fori_loop(0, TOK // 32, tally, 0)

    stat[...] = jnp.transpose(tcol[...])[:8, :]
    sends3 = [begin(remote(stat, gstat.at[k], es.at[k], er.at[k], {"ch": p})) for k, p in enumerate(others)]
    for copy in sends3:
        copy.wait_recv()
    parts = [stat[...]] + [gstat[k] for k in range(NCH - 1)]
    peak = parts[0][0:1, :]
    for v in parts[1:]:
        peak = jnp.maximum(peak, v[0:1, :])
    sum0 = sum1 = sum2 = picked = jnp.zeros((1, TOK), F32)
    for v in parts:
        d = v[0:1, :] - peak
        w = jnp.exp(d)
        wd = w * d
        sum0 = sum0 + w * v[1:2, :]
        sum1 = sum1 + (w * v[2:3, :] + wd * v[1:2, :])
        sum2 = sum2 + (w * v[3:4, :] + 2.0 * wd * v[2:3, :] + wd * d * v[1:2, :])
        picked = picked + v[4:5, :]
    log_total = jnp.log(sum0)
    ratio = sum1 / sum0
    out[0:1, :] = picked - peak - log_total
    out[1:2, :] = ratio - log_total
    out[2:3, :] = sum2 / sum0 - ratio * ratio
    out[3:8, :] = jnp.zeros((5, TOK), F32)

    for copy in pending:
        copy.wait_send()

    @pl.when(ctx < NCTX - 1)
    def _():
        remote(xin.at[pl.ds(TOK - 16, 16)], halo, halos.at[0], halor.at[0], {"ctx": after}).wait_send()

    for d in range(1, NZ):
        @pl.when(z + d < NZ)
        def _():
            for copy in pair(d, 1):
                copy.wait_send()
    for t in range(NT):
        for k in range(4):
            @pl.when(ch != 5 * k)
            def _():
                tile(t, k, ch, bcp, recvx, sx, rx).wait_send()

            @pl.when(ch == 5 * k)
            def _():
                for j in range(NCH - 1):
                    remote(
                        minex.at[t], bc.at[t, pl.ds(8 * k, 8)], sy.at[t, j], ry.at[t, k], {"ch": others[j]}
                    ).wait_send()


def tile(t, k, ch, bcp, recvx, sx, rx):
    where = lax.rem(ch - 5 * k + 2 * NCH, NCH) - 1
    return remote(bcp.at[t, pl.ds(8 * k, 8)], recvx.at[t, where], sx.at[t, k], rx.at[t, where], {"ch": 5 * k})


def per_device(
    layer_input, gate_input, conv_weight, conv_bias, select_weight, step_weight, step_bias, decay_log,
    skip_gain, out_weight, residual, norm_gain, head_weight, targets,
):
    n = NCH - 1
    dma = pltpu.SemaphoreType.DMA
    v = pltpu.VMEM
    result = pl.pallas_call(
        kernel,
        out_shape=jax.ShapeDtypeStruct((8, TOK), F32),
        in_specs=[HBM] * 6 + [VM] * 8,
        out_specs=VM,
        scratch_shapes=[
            v((TOK, CH), BF16), v((TOK, CH), BF16), v((RANK + 2 * STATE, CH), BF16), v((RANK, CH), BF16),
            v((CH, D), BF16), v((D, VOC), BF16), v((16, CH), BF16), v((TOK + 8, CH), F32), v((TOK, CH), BF16),
            v((TOK, CH), F32), v((STATE * 8, 128), F32),
            v((NT, RANK, TC), BF16), v((NT, 2 * STATE, TC), F32), v((NT, n, ROWS, TC), BF16), v((NT, ROWS, TC), BF16),
            v((NT, RANK, TC), BF16), v((NT, n, 8, TC), F32), v((NT, 8, TC), F32), v((NT, 2 * STATE, TC), F32),
            v((2 * STATE, TOK, 128), F32),
            v((FLAT, 128), F32), v((FLAT, 128), F32), v((STATE * 8, 128), F32), v((8, 128), F32),
            v((HALF, 128), F32), v((HALF, 128), F32), v((8, 128), F32),
            v((HALF, 128), BF16), v((8, 128), F32), v((NZ - 1, HALF, 128), BF16), v((NZ - 1, 8, 128), F32),
            v((HALF, 128), F32), v((HALF, 128), F32), v((STATE * 8, 128), F32),
            v((TOK, CH), BF16), v((NCH, TOK, BLK), F32), v((NCH, TOK, BLK), BF16), v((15, TOK, BLK), BF16),
            v((TOK, D), BF16), v((TOK, 1), F32), v((TOK, 128), F32), v((8, TOK), F32), v((n, 8, TOK), F32),
            dma((6,)), dma((2, 4, 2)), dma((2, 4, 2)), dma((2, 4, 2)), dma((2, 4, 2)), dma((1,)), dma((1,)),
            dma((NT, n)), dma((NT, n)), dma((NT, n)), dma((NT, n)),
            dma((NT, 4)), dma((NT, n)), dma((NT, n)), dma((NT, 4)),
            dma((2,)), dma((2,)), dma((2, NZ - 1)), dma((2, NZ - 1)), dma((1,)), dma((1,)),
            dma((NCH, NQ)), dma((15, NQ)), dma((NQ, 15)), dma((NQ, 15)), dma((n,)), dma((n,)),
        ],
        compiler_params=pltpu.CompilerParams(
            vmem_limit_bytes=67043328, collective_id=0, has_side_effects=True
        ),
        name="score_window",
    )(
        layer_input, gate_input, select_weight, step_weight, out_weight, head_weight, residual, conv_weight,
        conv_bias[None, :], step_bias[None, :], decay_log, skip_gain[None, :], norm_gain[None, :], targets[None, :],
    )
    return result[0], result[1], result[2]


def solution(mesh):
    in_specs = (
        P("ctx", "ch"), P("ctx", "ch"), P(None, "ch"), P("ch"), P(None, "ch"), P(None, "ch"), P("ch"),
        P(None, "ch"), P("ch"), P("ch", None), P("ctx", "ch"), P(), P("ctx", "ch"), P("ctx"),
    )
    return jax.shard_map(
        per_device, mesh=mesh, in_specs=in_specs, out_specs=(P("ctx"), P("ctx"), P("ctx")), check_vma=False
    )
```

```python
import jax
import jax.numpy as jnp
from jax import lax
from jax.experimental import pallas as pl
from jax.experimental.pallas import tpu as pltpu
from jax.sharding import PartitionSpec as P

STATE = 16
RANK = 512
KCONV = 4
TOK = 384
CH = 1024
D = 4096
VOC = 2048
NCH = 16
NCTX = 16
NZ = 8
NT = 3
TC = TOK // NT
ROWS = RANK // NCH
NTB = TOK // 8
FLAT = NTB * 64
HALF = STATE * 4
NK = 2
TK = TOK // NK
NQ = 4 * NK
QR = TOK // NQ
BLK = D // NCH
HB = D // NCTX
HP = HB // 2
VT = 256
NVT = VOC // VT
MESH = pl.DeviceIdType.MESH
F32 = jnp.float32
BF16 = jnp.bfloat16
VM = pl.BlockSpec(memory_space=pltpu.VMEM)
HBM = pl.BlockSpec(memory_space=pl.ANY)
SLOT = (0, 8, 12, 14)


def remote(src, dst, send_sem, recv_sem, peer):
    return pltpu.make_async_remote_copy(
        src_ref=src, dst_ref=dst, send_sem=send_sem, recv_sem=recv_sem, device_id=peer, device_id_type=MESH
    )


def sigmoid_linear(operand):
    return operand / (1.0 + jnp.exp(-operand))


def cube_of(index):
    x, y = index // 4, lax.rem(index, 4)
    return [lax.rem(x + x // 2, 2), x // 2, lax.rem(y + y // 2, 2), y // 2]


def index_of(bits):
    def line(low, high):
        return high * 2 + lax.rem(high + low, 2)

    return line(bits[0], bits[1]) * 4 + line(bits[2], bits[3])


def kernel(
    xin, gate_in, select_in, stepw_in, outw_in, head_in, residual, conv_w, conv_b, step_b, decay_in, skip, gain, targets,
    out,
    xs, gs, sel, stepw, wv, head, halo, xpad, sm, sg, dflat, pb, bcp, recv, mine, proj, recvx, minex, bc, bb,
    dtf, uf, state, total, swap_s, got_s, got_e, send_s, send_e, zs, ze, hold, fin, into,
    mixer, acc, part, got, scaled, rms, tcol, stat, gstat,
    ld, hs, hr, hps, hpr, halos, halor, s1, r1, s2, r2, sx, rx, sy, ry, cs, cr, csz, crz, csf, crf, ms, mr, gsn, grv, es, er,
):
    ch = lax.axis_index("ch")
    ctx = lax.axis_index("ctx")
    z, c = ctx // 2, lax.rem(ctx, 2)
    pending = []

    def begin(copy):
        copy.start()
        pending.append(copy)
        return copy

    others = [lax.rem(ch + off, NCH) for off in range(1, NCH)]
    partner = {"ctx": z * 2 + 1 - c}
    after, before = lax.rem(ctx + 1, NCTX), lax.rem(ctx + NCTX - 1, NCTX)
    cross = jnp.where(c == 0, before, after)
    greeted = [{"ch": p} for p in others] + [partner, {"ctx": cross}]
    greeted += [{"ctx": lax.rem(z + d, NZ) * 2 + c} for d in range(1, NZ)]
    barrier = pltpu.get_barrier_semaphore()
    for peer in greeted:
        pl.semaphore_signal(barrier, inc=1, device_id=peer, device_id_type=MESH)

    own = pl.ds(pl.multiple_of(ctx * HB, HB), HB)
    local = [
        pltpu.make_async_copy(xin, xs, ld.at[0]),
        pltpu.make_async_copy(select_in, sel, ld.at[1]),
        pltpu.make_async_copy(stepw_in, stepw, ld.at[2]),
        pltpu.make_async_copy(gate_in, gs, ld.at[3]),
        pltpu.make_async_copy(head_in, head.at[own], ld.at[4]),
        pltpu.make_async_copy(outw_in, wv, ld.at[5]),
    ]
    for copy in local:
        copy.start()
    pl.semaphore_wait(barrier, len(greeted))

    @pl.when(ctx < NCTX - 1)
    def _():
        remote(xin.at[pl.ds(TOK - 16, 16)], halo, halos.at[0], halor.at[0], {"ctx": after}).start()

    right = {"ctx": lax.rem(z + 1, NZ) * 2 + c}
    left = {"ctx": lax.rem(z + NZ - 1, NZ) * 2 + c}

    def rows_of(zb, core, p):
        start = pl.multiple_of((zb * 2 + core) * HB + p * HP, HP)
        return head.at[pl.ds(start, HP)]

    def hop(way, k, p):
        zb = lax.rem(z + NZ - k, NZ) if way == 0 else lax.rem(z + k, NZ)
        where = rows_of(zb, c, p)
        src = head_in.at[pl.ds(p * HP, HP)] if k == 0 else where
        return remote(src, where, hs.at[way, k, p], hr.at[way, k, p], right if way == 0 else left)

    def arrival(way, k, p):
        zb = lax.rem(z + NZ - 1 - k, NZ) if way == 0 else lax.rem(z + 1 + k, NZ)
        where = rows_of(zb, c, p)
        return remote(where, where, hs.at[way, k, p], hr.at[way, k, p], right if way == 0 else left), where

    def valid(way, k, p):
        return k < 3 or (k == 3 and p == way)

    def relay(k, p):
        for way in range(2):
            if valid(way, k, p):
                arrival(way, k, p)[0].wait_recv()
                if valid(way, k + 1, p):
                    begin(hop(way, k + 1, p))

    def share(k, p):
        for way in range(2):
            if valid(way, k, p):
                where = arrival(way, k, p)[1]
                begin(remote(where, where, hps.at[way, k, p], hpr.at[way, k, p], partner))

    def pump(k, p):
        relay(k, p)
        share(k, p)

    for p in range(2):
        for way in range(2):
            begin(hop(way, 0, p))
    mine_rows = head.at[own]
    begin(remote(head_in, mine_rows, hps.at[0, 3, 1], hpr.at[0, 3, 1], partner))

    for lt in range(8):
        lanes = slice(128 * lt, 128 * lt + 128)
        for h in range(2):
            dflat[pl.ds(lt + 64 * h, 8, stride=8), :] = decay_in[8 * h : 8 * h + 8, lanes]
    local[0].wait()
    for k in range(TOK // 32):
        xpad[8 + 32 * k : 40 + 32 * k, :] = xs[32 * k : 32 * k + 32, :].astype(F32)

    @pl.when(ctx > 0)
    def _():
        remote(xin.at[pl.ds(TOK - 16, 16)], halo, halos.at[0], halor.at[0], {"ctx": after}).wait_recv()
        xpad[0:8, :] = halo[...].astype(F32)[8:16, :]

    @pl.when(ctx == 0)
    def _():
        xpad[0:8, :] = jnp.zeros((8, CH), F32)

    local[1].wait()
    sends1 = {}

    def convolve(t):
        for k in range(TC // 32):
            r0 = TC * t + 32 * k
            for half in range(2):
                lanes = slice(512 * half, 512 * half + 512)
                v = jnp.zeros((32, 512), F32) + conv_b[:, lanes]
                for offset in range(KCONV):
                    v = v + conv_w[offset : offset + 1, lanes] * xpad[r0 + 5 + offset : r0 + 37 + offset, lanes]
                sm[r0 : r0 + 32, lanes] = sigmoid_linear(v).astype(BF16)

    for t in range(NT):
        pl.when(ch >= 0)(lambda: convolve(t))
        product = lax.dot_general(
            sel[...], sm[TC * t : TC * t + TC, :], (((1,), (1,)), ((), ())), preferred_element_type=F32
        )
        pb[t] = product[:RANK].astype(BF16)
        bcp[t] = product[RANK:]
        for k, p in enumerate(others):
            rows = pl.ds(pl.multiple_of(p * ROWS, ROWS), ROWS)
            sends1[t, k] = begin(remote(pb.at[t, rows], recv.at[t, k], s1.at[t, k], r1.at[t, k], {"ch": p}))
        for k in range(4):
            @pl.when(ch != 5 * k)
            def _():
                tile(t, k, ch, bcp, recvx, sx, rx).start()

    local[3].wait()
    for k in range(TOK // 32):
        sg[32 * k : 32 * k + 32, :] = sigmoid_linear(gs[32 * k : 32 * k + 32, :].astype(F32))

    myrows = pl.ds(pl.multiple_of(ch * ROWS, ROWS), ROWS)
    sends2 = {}
    for t in range(NT):
        for k in range(NCH - 1):
            sends1[t, k].wait_recv()
        summed = pb[t, myrows].astype(F32)
        for k in range(NCH - 1):
            summed = summed + recv[t, k].astype(F32)
        mine[t] = summed.astype(BF16)
        for k, p in enumerate(others):
            sends2[t, k] = begin(remote(mine.at[t], proj.at[t, myrows], s2.at[t, k], r2.at[t, k], {"ch": p}))
        proj[t, myrows] = mine[t]
        for k in range(4):
            @pl.when(ch == 5 * k)
            def _():
                sumx = bcp[t, 8 * k : 8 * k + 8]
                for j in range(NCH - 1):
                    remote(minex.at[t], recvx.at[t, j], sx.at[t, 0], rx.at[t, j], {"ch": others[0]}).wait_recv()
                    sumx = sumx + recvx[t, j]
                minex[t] = sumx
                for j in range(NCH - 1):
                    remote(
                        minex.at[t], bc.at[t, pl.ds(8 * k, 8)], sy.at[t, j], ry.at[t, k], {"ch": others[j]}
                    ).start()
                bc[t, 8 * k : 8 * k + 8] = minex[t]

    pump(0, 0)

    local[2].wait()
    rates = [-jnp.exp(dflat[8 * n : 8 * n + 8, :]) for n in range(STATE)]
    carry = (jnp.zeros((8, 128), F32),) * (STATE + 1)
    for t in range(NT):
        for k in range(NCH - 1):
            sends2[t, k].wait_recv()
        for k in range(4):
            @pl.when(ch != 5 * k)
            def _():
                remote(minex.at[t], bc.at[t, pl.ds(8 * k, 8)], sy.at[t, 0], ry.at[t, k], {"ch": 5 * k}).wait_recv()

        turned = jnp.transpose(bc[t])
        for n in range(2 * STATE):
            bb[n, TC * t : TC * t + TC, :] = jnp.broadcast_to(turned[:, n : n + 1], (TC, 128))
        raw = lax.dot_general(proj[t], stepw[...], (((0,), (0,)), ((), ())), preferred_element_type=F32)
        v = raw + step_b[...]
        dt = jnp.maximum(v, 0.0) + jnp.log1p(jnp.exp(-jnp.abs(v)))
        u = dt * sm[TC * t : TC * t + TC, :].astype(F32)
        for b in range(TC // 8):
            for lt in range(8):
                start = (TC // 8 * t + b) * 64 + lt * 8
                dtf[start : start + 8, :] = dt[8 * b : 8 * b + 8, 128 * lt : 128 * lt + 128]
                uf[start : start + 8, :] = u[8 * b : 8 * b + 8, 128 * lt : 128 * lt + 128]

        def step(tb, held):
            s, elapsed = list(held[:STATE]), held[STATE]
            for r in range(8):
                rows = pl.ds(tb * 64 + r, 8, stride=8)
                dt = dtf[rows, :]
                u = uf[rows, :]
                splat = pl.ds(tb * 8 + r, 8, stride=0)
                y = None
                for n in range(STATE):
                    s[n] = jnp.exp(dt * rates[n]) * s[n] + u * bb[n, splat, :]
                    term = s[n] * bb[STATE + n, splat, :]
                    y = term if y is None else y + term
                elapsed = elapsed + dt
                uf[rows, :] = y
                dtf[rows, :] = elapsed
            return (*s, elapsed)

        carry = lax.fori_loop(TC // 8 * t, TC // 8 * (t + 1), step, carry)
    for n in range(STATE):
        state[8 * n : 8 * n + 8, :] = carry[n]
    total[...] = carry[STATE]

    half = pl.ds(pl.multiple_of(c * HALF, HALF), HALF)
    other = pl.ds(pl.multiple_of((1 - c) * HALF, HALF), HALF)
    swap_s[...] = state[other, :]
    a = begin(remote(swap_s, got_s, cs.at[0], cr.at[0], partner))
    b = begin(remote(total, got_e, cs.at[1], cr.at[1], partner))
    rate = -jnp.exp(dflat[half, :])

    def through(elapsed):
        return jnp.exp(rate * jnp.tile(elapsed, (HALF // 8, 1)))

    a.wait_recv()
    b.wait_recv()
    own_s, own_e, oth_s, oth_e = state[half, :], total[...], got_s[...], got_e[...]
    low = c == 0
    t0, t1 = jnp.where(low, own_s, oth_s), jnp.where(low, oth_s, own_s)
    e0, e1 = jnp.where(low, own_e, oth_e), jnp.where(low, oth_e, own_e)
    send_s[...] = (through(e1) * t0 + t1).astype(send_s.dtype)
    send_e[...] = e0 + e1

    def pair(d, sign):
        peer = {"ctx": (z + sign * d) * 2 + c}
        return (
            remote(send_s, zs.at[d - 1], csz.at[0, d - 1], crz.at[0, d - 1], peer),
            remote(send_e, ze.at[d - 1], csz.at[1, d - 1], crz.at[1, d - 1], peer),
        )

    for d in range(1, NZ):
        @pl.when(z + d < NZ)
        def _():
            for copy in pair(d, 1):
                copy.start()

    relay(0, 1)
    hold[...] = jnp.zeros_like(hold)
    for d in range(NZ - 1, 0, -1):
        @pl.when(z >= d)
        def _():
            for copy in pair(d, -1):
                copy.wait_recv()
            hold[...] = through(ze[d - 1]) * hold[...] + zs[d - 1].astype(F32)

    into0 = hold[...]
    into1 = through(e0) * into0 + t0
    fin[...] = jnp.where(low, into1, into0)
    into[half, :] = jnp.where(low, into0, into1)
    f = begin(remote(fin, into.at[half], csf.at[0], crf.at[0], partner))
    f.wait_recv()
    relay(1, 0)
    share(0, 1)
    share(1, 0)

    came = [into[8 * n : 8 * n + 8, :] for n in range(STATE)]

    def fix(tb, _):
        for r in range(8):
            rows = pl.ds(tb * 64 + r, 8, stride=8)
            elapsed = dtf[rows, :]
            y = uf[rows, :]
            splat = pl.ds(tb * 8 + r, 8, stride=0)
            for n in range(STATE):
                y = y + jnp.exp(elapsed * rates[n]) * came[n] * bb[STATE + n, splat, :]
            uf[rows, :] = y
        return 0

    def gate_chunk(ck):
        lax.fori_loop(NTB // NK * ck, NTB // NK * (ck + 1), fix, 0)
        for k in range(TK // 16 * ck, TK // 16 * (ck + 1)):
            rows = slice(16 * k, 16 * k + 16)
            for lt in range(8):
                lanes = slice(128 * lt, 128 * lt + 128)
                start = (2 * k) * 64 + lt * 8
                scanned = jnp.concatenate([uf[start : start + 8, :], uf[start + 64 : start + 72, :]], axis=0)
                value = scanned + skip[:, lanes] * sm[rows, lanes].astype(F32)
                mixer[rows, lanes] = (value * sg[rows, lanes]).astype(BF16)

    bits = cube_of(ch)

    def block(r):
        return index_of([lax.rem(bits[d] + ((r >> d) & 1), 2) for d in range(4)])

    def lanes_of(r):
        return pl.ds(pl.multiple_of(block(r) * BLK, BLK), BLK)

    peers = [{"ch": block(1 << d)} for d in range(4)]

    def rows(q):
        return pl.ds(QR * q, QR)

    def dim(q, s):
        return (q + s) % 4

    def kept(q, s):
        return [r for r in range(16) if all(not (r >> dim(q, i)) & 1 for i in range(s))]

    def slot(q, s, r):
        return SLOT[s] + kept(q, s + 1).index(r)

    def send(q, s, r):
        d = dim(q, s)
        k = slot(q, s, r ^ (1 << d))
        begin(remote(part.at[r, rows(q)], got.at[k, rows(q)], ms.at[r, q], mr.at[k, q], peers[d]))

    def take(q, s, r):
        k = slot(q, s, r)
        remote(part.at[r, rows(q)], got.at[k, rows(q)], ms.at[r, q], mr.at[k, q], peers[dim(q, s)]).wait_recv()
        return got[k, rows(q)].astype(F32)

    def groups(ck):
        return range(4 * ck, 4 * ck + 4)

    def multiply(ck):
        here = slice(TK * ck, TK * ck + TK)
        for r in [15, 14, 13, 11, 7, 12, 10, 9, 6, 5, 3, 8, 4, 2, 1, 0]:
            product = jnp.dot(mixer[here, :], wv[:, lanes_of(r)], preferred_element_type=F32)
            acc[r, here] = product
            part[r, here] = product.astype(BF16)
            for q in groups(ck):
                if (r >> dim(q, 0)) & 1:
                    send(q, 0, r)

    def fold(ck, s):
        for q in groups(ck):
            left_over = kept(q, s + 1)
            d = dim(q, s + 1)
            for r in [r for r in left_over if (r >> d) & 1] + [r for r in left_over if not (r >> d) & 1]:
                value = acc[r, rows(q)] + take(q, s, r)
                if (r >> d) & 1:
                    part[r, rows(q)] = value.astype(BF16)
                    send(q, s + 1, r)
                else:
                    acc[r, rows(q)] = value

    def spread(q, s):
        held = [0]
        for i in range(s):
            held = held + [r ^ (1 << dim(q, i)) for r in held]
        return held

    def give(q, s, r):
        k = (1 << s) - 1 + spread(q, s).index(r)
        where = scaled.at[rows(q), lanes_of(r)]
        begin(remote(where, where, gsn.at[q, k], grv.at[q, k], peers[dim(q, s)]))

    def finish(ck):
        for q in groups(ck):
            hidden = residual[rows(q), :].astype(F32) + (acc[0, rows(q)] + take(q, 3, 0))
            scaled[rows(q), lanes_of(0)] = (hidden * gain[:, lanes_of(0)]).astype(BF16)
            give(q, 0, 0)

    def widen(ck, s):
        for q in groups(ck):
            for r in spread(q, s):
                k = (1 << s) - 1 + spread(q, s).index(r)
                where = scaled.at[rows(q), lanes_of(r ^ (1 << dim(q, s)))]
                remote(where, where, gsn.at[q, k], grv.at[q, k], peers[dim(q, s)]).wait_recv()
            if s < 3:
                for r in spread(q, s + 1):
                    give(q, s + 1, r)

    def logits(ck):
        here = slice(TK * ck, TK * ck + TK)

        def square(k, held):
            where = pl.ds(pl.multiple_of(k * BLK, BLK), BLK)
            h = scaled[here, where].astype(F32) / gain[:, where]
            acc[8, here] += h * h
            return held

        acc[8, here] = jnp.zeros((TK, BLK), F32)
        lax.fori_loop(0, NCH, square, 0)
        rms[here, :] = lax.rsqrt(jnp.sum(acc[8, here], axis=1, keepdims=True) * (1.0 / D) + 1e-06)

        def logit(j, held):
            where = pl.ds(pl.multiple_of(j * VT, VT), VT)
            value = None
            for i in (0, 1, 7, 2, 6, 3, 5):
                product = chip_part(here, where, i)
                value = product if value is None else value + product
            acc[j, here] = value
            return held

        lax.fori_loop(0, NVT, logit, 0)

    def chip_part(here, where, i):
        deep = pl.ds(pl.multiple_of(lax.rem(z + i, NZ) * 2 * HB, 2 * HB), 2 * HB)
        return jnp.dot(scaled[here, deep], head[deep, where], preferred_element_type=F32)

    def last_part(j, held):
        where = pl.ds(pl.multiple_of(j * VT, VT), VT)
        acc[j] = (acc[j] + chip_part(slice(0, TOK), where, 4)) * rms[...]
        return held

    def shared(k, p):
        for way in range(2):
            if valid(way, k, p):
                where = head.at[pl.ds(0, HP)]
                remote(where, where, hps.at[way, k, p], hpr.at[way, k, p], partner).wait_recv()

    gate_chunk(0)
    local[5].wait()
    multiply(0)
    gate_chunk(1)
    pump(1, 1)
    fold(0, 0)
    multiply(1)
    fold(0, 1)
    fold(1, 0)
    fold(0, 2)
    fold(1, 1)
    finish(0)
    pump(2, 0)
    fold(1, 2)
    widen(0, 0)
    finish(1)
    widen(0, 1)
    pump(2, 1)
    widen(1, 0)
    widen(0, 2)
    widen(1, 1)
    widen(1, 2)
    widen(0, 3)

    local[4].wait()
    for k in range(3):
        for p in range(2):
            shared(k, p)
    remote(head_in, mine_rows, hps.at[0, 3, 1], hpr.at[0, 3, 1], partner).wait_recv()
    logits(0)
    widen(1, 3)
    logits(1)
    for p in range(2):
        pump(3, p)
    for p in range(2):
        shared(3, p)
    lax.fori_loop(0, NVT, last_part, 0)
    tcol[...] = jnp.transpose(jnp.broadcast_to((targets[...].reshape(1, TOK) - ch * VOC).astype(F32), (128, TOK)))
    lane = lax.broadcasted_iota(jnp.int32, (32, VT), 1).astype(F32)
    place = lax.broadcasted_iota(jnp.int32, (32, 128), 1)

    def tally(k, held):
        here = pl.ds(pl.multiple_of(k * 32, 32), 32)
        values = [acc[j, here] for j in range(NVT)]
        peak = values[0]
        for v in values[1:]:
            peak = jnp.maximum(peak, v)
        peak = jnp.max(peak, axis=1, keepdims=True)
        want = tcol[here, :][:, 0:1]
        sums = [jnp.zeros((32, VT), F32) for _ in range(4)]
        for j, v in enumerate(values):
            shifted = v - peak
            w = jnp.exp(shifted)
            ws = w * shifted
            sums[0] = sums[0] + w
            sums[1] = sums[1] + ws
            sums[2] = sums[2] + ws * shifted
            sums[3] = sums[3] + jnp.where(lane + float(j * VT) == want, v, 0.0)
        cols = [peak] + [jnp.sum(v, axis=1, keepdims=True) for v in sums]
        packed = jnp.zeros((32, 128), F32)
        for i, v in enumerate(cols):
            packed = jnp.where(place == i, v, packed)
        tcol[here, :] = packed
        return held

    lax.fori_loop(0, TOK // 32, tally, 0)

    stat[...] = jnp.transpose(tcol[...])[:8, :]
    sends3 = [begin(remote(stat, gstat.at[k], es.at[k], er.at[k], {"ch": p})) for k, p in enumerate(others)]
    for copy in sends3:
        copy.wait_recv()
    parts = [stat[...]] + [gstat[k] for k in range(NCH - 1)]
    peak = parts[0][0:1, :]
    for v in parts[1:]:
        peak = jnp.maximum(peak, v[0:1, :])
    sum0 = sum1 = sum2 = picked = jnp.zeros((1, TOK), F32)
    for v in parts:
        d = v[0:1, :] - peak
        w = jnp.exp(d)
        wd = w * d
        sum0 = sum0 + w * v[1:2, :]
        sum1 = sum1 + (w * v[2:3, :] + wd * v[1:2, :])
        sum2 = sum2 + (w * v[3:4, :] + 2.0 * wd * v[2:3, :] + wd * d * v[1:2, :])
        picked = picked + v[4:5, :]
    log_total = jnp.log(sum0)
    ratio = sum1 / sum0
    out[0:1, :] = picked - peak - log_total
    out[1:2, :] = ratio - log_total
    out[2:3, :] = sum2 / sum0 - ratio * ratio
    out[3:8, :] = jnp.zeros((5, TOK), F32)

    for copy in pending:
        copy.wait_send()

    @pl.when(ctx < NCTX - 1)
    def _():
        remote(xin.at[pl.ds(TOK - 16, 16)], halo, halos.at[0], halor.at[0], {"ctx": after}).wait_send()

    for d in range(1, NZ):
        @pl.when(z + d < NZ)
        def _():
            for copy in pair(d, 1):
                copy.wait_send()
    for t in range(NT):
        for k in range(4):
            @pl.when(ch != 5 * k)
            def _():
                tile(t, k, ch, bcp, recvx, sx, rx).wait_send()

            @pl.when(ch == 5 * k)
            def _():
                for j in range(NCH - 1):
                    remote(
                        minex.at[t], bc.at[t, pl.ds(8 * k, 8)], sy.at[t, j], ry.at[t, k], {"ch": others[j]}
                    ).wait_send()


def tile(t, k, ch, bcp, recvx, sx, rx):
    where = lax.rem(ch - 5 * k + 2 * NCH, NCH) - 1
    return remote(bcp.at[t, pl.ds(8 * k, 8)], recvx.at[t, where], sx.at[t, k], rx.at[t, where], {"ch": 5 * k})


def per_device(
    layer_input, gate_input, conv_weight, conv_bias, select_weight, step_weight, step_bias, decay_log,
    skip_gain, out_weight, residual, norm_gain, head_weight, targets,
):
    n = NCH - 1
    dma = pltpu.SemaphoreType.DMA
    v = pltpu.VMEM
    result = pl.pallas_call(
        kernel,
        out_shape=jax.ShapeDtypeStruct((8, TOK), F32),
        in_specs=[HBM] * 6 + [VM] * 8,
        out_specs=VM,
        scratch_shapes=[
            v((TOK, CH), BF16), v((TOK, CH), BF16), v((RANK + 2 * STATE, CH), BF16), v((RANK, CH), BF16),
            v((CH, D), BF16), v((D, VOC), BF16), v((16, CH), BF16), v((TOK + 8, CH), F32), v((TOK, CH), BF16),
            v((TOK, CH), F32), v((STATE * 8, 128), F32),
            v((NT, RANK, TC), BF16), v((NT, 2 * STATE, TC), F32), v((NT, n, ROWS, TC), BF16), v((NT, ROWS, TC), BF16),
            v((NT, RANK, TC), BF16), v((NT, n, 8, TC), F32), v((NT, 8, TC), F32), v((NT, 2 * STATE, TC), F32),
            v((2 * STATE, TOK, 128), F32),
            v((FLAT, 128), F32), v((FLAT, 128), F32), v((STATE * 8, 128), F32), v((8, 128), F32),
            v((HALF, 128), F32), v((HALF, 128), F32), v((8, 128), F32),
            v((HALF, 128), BF16), v((8, 128), F32), v((NZ - 1, HALF, 128), BF16), v((NZ - 1, 8, 128), F32),
            v((HALF, 128), F32), v((HALF, 128), F32), v((STATE * 8, 128), F32),
            v((TOK, CH), BF16), v((NCH, TOK, BLK), F32), v((NCH, TOK, BLK), BF16), v((15, TOK, BLK), BF16),
            v((TOK, D), BF16), v((TOK, 1), F32), v((TOK, 128), F32), v((8, TOK), F32), v((n, 8, TOK), F32),
            dma((6,)), dma((2, 4, 2)), dma((2, 4, 2)), dma((2, 4, 2)), dma((2, 4, 2)), dma((1,)), dma((1,)),
            dma((NT, n)), dma((NT, n)), dma((NT, n)), dma((NT, n)),
            dma((NT, 4)), dma((NT, n)), dma((NT, n)), dma((NT, 4)),
            dma((2,)), dma((2,)), dma((2, NZ - 1)), dma((2, NZ - 1)), dma((1,)), dma((1,)),
            dma((NCH, NQ)), dma((15, NQ)), dma((NQ, 15)), dma((NQ, 15)), dma((n,)), dma((n,)),
        ],
        compiler_params=pltpu.CompilerParams(
            vmem_limit_bytes=67043328, collective_id=0, has_side_effects=True
        ),
        name="score_window",
    )(
        layer_input, gate_input, select_weight, step_weight, out_weight, head_weight, residual, conv_weight,
        conv_bias[None, :], step_bias[None, :], decay_log, skip_gain[None, :], norm_gain[None, :], targets,
    )
    return result[0], result[1], result[2]


def solution(mesh):
    in_specs = (
        P("ctx", "ch"), P("ctx", "ch"), P(None, "ch"), P("ch"), P(None, "ch"), P(None, "ch"), P("ch"),
        P(None, "ch"), P("ch"), P("ch", None), P("ctx", "ch"), P(), P("ctx", "ch"), P("ctx"),
    )
    return jax.shard_map(
        per_device, mesh=mesh, in_specs=in_specs, out_specs=(P("ctx"), P("ctx"), P("ctx")), check_vma=False
    )
```
